128 devices in a mesh: row: 8 (over y, core), col: 16 (over z, x).
Axes of the slice: x: 4, y: 4, z: 4, core: 2. Of those that a mesh axis runs over, the one named last changes fastest.
Arguments:
- rhs: float32 [64, 65536], P(None, ('row', 'col')), may hold values from -6 to 6
- self_term: float32 [65536], P(('row', 'col')), may hold values from 4 to 6
- near_tiles: bfloat16 [16384, 256, 256], P(('row', 'col')), may hold values from -0.0241 to 0.0241
- near_rows: int32 [16384], P(('row', 'col')), may hold values from 0 to 31
- near_cols: int32 [16384], P(('row', 'col')), may hold values from 0 to 15
- near_counts: int32 [128], replicated, may hold values from 1 to 128, as said below
- far_left: bfloat16 [8192, 256, 32], P(('row', 'col')), may hold values from -0.125 to 0.125
- far_right: bfloat16 [8192, 256, 32], P(('row', 'col')), may hold values from -0.125 to 0.125
- far_rows: int32 [8192], P(('row', 'col')), may hold values from 0 to 31
- far_cols: int32 [8192], P(('row', 'col')), may hold values from 0 to 15
- nys_factor: float32 [512, 65536], P(None, ('row', 'col')), may hold values from -0.0234375 to 0.0234375
- nys_weight: float32 [512], replicated, may hold values from 1 to 16
Outputs:
- solution: float32 [64, 65536], P(None, ('row', 'col'))
- residual: float32 [64, 65536], P(None, ('row', 'col'))
The draws below stay inside these ranges and needn't reach their ends.
Inputs may be any that keep to these rules, and one draw needn't show every extreme that they name: Owner o uses its first near_counts[o] slots; some owner uses all 128.
All inputs are finite; a program needn't handle non-finite values.
Results may differ from the reference program's by a relative error of at most 0.0003.
Values may be sent and summed in bfloat16 or wider, within the bound.
A program may use at most 128 MiB of HBM per device.

```python
import math
import jax
import jax.numpy as jnp
from jax import lax

BLK = 256
RHS = 64
RANK = 512
PRANK = 32
BLOCKS_DEV = 2
NEAR_MAX = 128
FAR_DEV = 64
ITERS = 2
OWNERS = 128
ORDER = 65536
SLOTS = 16384
FAR_SLOTS = 8192
ROW_BLOCKS = 32
COL_BLOCKS = 16
N_COL = 16


def draw_near_tiles(key, part):
    values = 0.008 * jnp.clip(jax.random.normal(key, (SLOTS, BLK, BLK), jnp.float32), -3.0, 3.0)
    return values.astype(jnp.bfloat16)


def draw_near_counts(key, part):
    first = jax.random.randint(jax.random.fold_in(key, 11), (OWNERS,), 1, NEAR_MAX + 1)
    second = jax.random.randint(jax.random.fold_in(key, 12), (OWNERS,), 1, NEAR_MAX + 1)
    counts = 1 + (first * second - 1) // NEAR_MAX
    busiest = jax.random.randint(jax.random.fold_in(key, 13), (), 0, OWNERS)
    owners = jnp.arange(OWNERS, dtype=jnp.int32)
    return jnp.where(owners == busiest, NEAR_MAX, counts).astype(jnp.int32)


def place_ends(result, key, least, largest):
    longest = result.shape.index(max(result.shape))
    spots = []
    for shift in (0, 1):
        where = [jax.random.randint(jax.random.fold_in(key, axis), (), 0, length) for axis, length in enumerate(result.shape)]
        where[longest] = (where[longest] + shift) % result.shape[longest]
        spots.append(tuple(where))
    return result.at[spots[0]].set(least).at[spots[1]].set(largest)


def steps_of(stream_key, extent, pieces, smallest, top_value):
    gain, own = 1.0, jax.random.fold_in(stream_key, 6)
    for dim, blocks in pieces:
        steps = jnp.exp(jax.random.uniform(jax.random.fold_in(own, dim), (blocks,), jnp.float32, smallest / len(pieces), top_value / len(pieces)))
        gain = gain * jnp.repeat(steps, extent[dim] // blocks).reshape([-1 if axis == dim else 1 for axis in range(len(extent))])
    return gain


def gaussian(stream_key, extent, width, limit, split=(), kind=jnp.bfloat16):
    array = width * jax.random.normal(stream_key, extent, jnp.float32)
    if split:
        array = array * steps_of(stream_key, extent, split, -0.22, 0.18)
    return jnp.clip(array, -limit, limit).astype(kind)


def setup_inputs(seed: int = 0) -> dict:
    key_of = jax.random.split(jax.random.key(seed), 13)
    return {
        "rhs": gaussian(key_of[0], (RHS, ORDER), 1.0, 6.0, ((1, 128),), jnp.float32),
        "self_term": jnp.clip(4.0 + 2.0 * jax.random.uniform(key_of[1], (ORDER,), jnp.float32) ** steps_of(key_of[1], (ORDER,), ((0, 128),), -0.2, 0.2), 4.0, 6.0),
        "near_tiles": draw_near_tiles(jax.random.fold_in(key_of[12], 71), 0),
        "near_rows": place_ends(jax.random.randint(key_of[3], (SLOTS,), 0, ROW_BLOCKS), jax.random.fold_in(key_of[3], 1), 0, ROW_BLOCKS - 1).astype(jnp.int32),
        "near_cols": place_ends(jax.random.randint(key_of[4], (SLOTS,), 0, COL_BLOCKS), jax.random.fold_in(key_of[4], 1), 0, COL_BLOCKS - 1).astype(jnp.int32),
        "near_counts": draw_near_counts(jax.random.fold_in(key_of[12], 71), 0),
        "far_left": gaussian(key_of[6], (FAR_SLOTS, BLK, PRANK), 0.02, 0.125, ((0, 128),)),
        "far_right": gaussian(key_of[7], (FAR_SLOTS, BLK, PRANK), 0.02, 0.125, ((0, 128),)),
        "far_rows": place_ends(jax.random.randint(key_of[8], (FAR_SLOTS,), 0, ROW_BLOCKS), jax.random.fold_in(key_of[8], 1), 0, ROW_BLOCKS - 1).astype(jnp.int32),
        "far_cols": place_ends(jax.random.randint(key_of[9], (FAR_SLOTS,), 0, COL_BLOCKS), jax.random.fold_in(key_of[9], 1), 0, COL_BLOCKS - 1).astype(jnp.int32),
        "nys_factor": gaussian(key_of[10], (RANK, ORDER), ORDER ** -0.5, 0.0234375, ((1, 128),), jnp.float32),
        "nys_weight": jnp.clip(jnp.exp(jax.random.uniform(key_of[11], (RANK,), jnp.float32, math.log(1.0), math.log(16.0))), 1.0, 16.0),
    }


def place_blocks(owner, rows, cols):
    grid_row = owner // N_COL
    grid_col = owner % N_COL
    row_glob = grid_row * ROW_BLOCKS + rows
    col_glob = (cols // BLOCKS_DEV * N_COL + grid_col) * BLOCKS_DEV + cols % BLOCKS_DEV
    return (row_glob.astype(jnp.int32), col_glob.astype(jnp.int32))

def operate(direc, self_term, near_tiles, near_rows, near_cols, near_counts, far_left, far_right, far_rows, far_cols):
    nblocks = ORDER // BLK
    blocks = direc.astype(jnp.bfloat16).reshape(RHS, nblocks, BLK).transpose(1, 0, 2).astype(jnp.float32)
    owners = jnp.arange(OWNERS, dtype=jnp.int32)
    slot_ids = jnp.arange(NEAR_MAX, dtype=jnp.int32)

    def near_step(acc, item):
        owner, tiles, rows, cols = item
        row_glob, col_glob = place_blocks(owner, rows, cols)
        mask = (slot_ids < near_counts[owner])[:, None, None]
        tile_f = tiles.astype(jnp.float32)
        forward = jnp.einsum('smk,snk->smn', blocks[col_glob], tile_f)
        transposed = jnp.einsum('smn,snk->smk', blocks[row_glob], tile_f)
        acc = acc.at[row_glob].add(jnp.where(mask, forward, 0.0))
        acc = acc.at[col_glob].add(jnp.where(mask, transposed, 0.0))
        return (acc, None)

    def far_step(acc, item):
        owner, left, right, rows, cols = item
        row_glob, col_glob = place_blocks(owner, rows, cols)
        left_f = left.astype(jnp.float32)
        right_f = right.astype(jnp.float32)
        half_f = jnp.einsum('smk,skr->smr', blocks[col_glob], right_f).astype(jnp.bfloat16)
        half_t = jnp.einsum('smn,snr->smr', blocks[row_glob], left_f).astype(jnp.bfloat16)
        half_f, half_t = lax.optimization_barrier((half_f, half_t))
        forward = jnp.einsum('smr,snr->smn', half_f.astype(jnp.float32), left_f)
        transposed = jnp.einsum('smr,skr->smk', half_t.astype(jnp.float32), right_f)
        acc = acc.at[row_glob].add(forward)
        acc = acc.at[col_glob].add(transposed)
        return (acc, None)
    acc = jnp.zeros((nblocks, RHS, BLK), jnp.float32)
    acc, _ = lax.scan(near_step, acc, (owners, near_tiles.reshape(OWNERS, NEAR_MAX, BLK, BLK), near_rows.reshape(OWNERS, NEAR_MAX), near_cols.reshape(OWNERS, NEAR_MAX)))
    acc, _ = lax.scan(far_step, acc, (owners, far_left.reshape(OWNERS, FAR_DEV, BLK, PRANK), far_right.reshape(OWNERS, FAR_DEV, BLK, PRANK), far_rows.reshape(OWNERS, FAR_DEV), far_cols.reshape(OWNERS, FAR_DEV)))
    return self_term * direc + acc.transpose(1, 0, 2).reshape(RHS, ORDER)

def precondition(resid, nys_factor, nys_weight):
    proj = jnp.dot(resid, nys_factor.T, precision=lax.Precision.HIGHEST)
    return resid + jnp.dot(proj * nys_weight, nys_factor, precision=lax.Precision.HIGHEST)

def chol_solve(matrix, target):
    return jax.scipy.linalg.cho_solve((jnp.linalg.cholesky(matrix), True), target)

def reference(rhs, self_term, near_tiles, near_rows, near_cols, near_counts, far_left, far_right, far_rows, far_cols, nys_factor, nys_weight):
    hp = lax.Precision.HIGHEST
    solution = jnp.zeros_like(rhs)
    residual = rhs
    precond = precondition(residual, nys_factor, nys_weight)
    rho = jnp.dot(residual, precond.T, precision=hp)
    direc = precond
    for step in range(ITERS):
        image = operate(direc, self_term, near_tiles, near_rows, near_cols, near_counts, far_left, far_right, far_rows, far_cols)
        gram = jnp.dot(direc, image.T, precision=hp)
        alpha = chol_solve(gram, rho)
        solution = solution + jnp.dot(alpha.T, direc, precision=hp)
        residual = residual - jnp.dot(alpha.T, image, precision=hp)
        if step + 1 < ITERS:
            precond = precondition(residual, nys_factor, nys_weight)
            rho_next = jnp.dot(residual, precond.T, precision=hp)
            beta = chol_solve(rho, rho_next)
            direc = precond + jnp.dot(beta.T, direc, precision=hp)
            rho = rho_next
    return (solution, residual)
```

```python
import functools

import jax
import jax.numpy as jnp
from jax import lax
from jax.experimental import pallas as pl
from jax.experimental.pallas import tpu as pltpu
from jax.sharding import PartitionSpec as P

MESH = pl.DeviceIdType.MESH
HI = lax.Precision.HIGHEST
F32 = jnp.float32
BF16 = jnp.bfloat16
VMEM = pl.BlockSpec(memory_space=pltpu.VMEM)
SMEM = pl.BlockSpec(memory_space=pltpu.SMEM)
ANY = pl.BlockSpec(memory_space=pl.ANY)
NT = (((1,), (1,)), ((), ()))
NN = (((1,), (0,)), ((), ()))
TN = (((0,), (0,)), ((), ()))
M = 64
B = 256
D = 512
WIDE = 640
GROUP = 8


def dot(a, b, dims=NN, precision=None):
    return lax.dot_general(a, b, dims, precision=precision, preferred_element_type=F32)


class Net:
    def __init__(self, send, recv):
        self.send, self.recv, self.used = send, recv, 0
        self.i, self.j = lax.axis_index("row"), lax.axis_index("col")
        self.y, self.core = self.i // 2, self.i % 2
        self.z, self.x = self.j // 4, self.j % 4

    def partner(self):
        return (self.y * 2 + 1 - self.core, self.j)

    def at(self, axis, step):
        if axis == "y":
            return ((self.y + step) % 4 * 2 + self.core, self.j)
        if axis == "z":
            return (self.i, (self.z + step) % 4 * 4 + self.x)
        return (self.i, self.z * 4 + (self.x + step) % 4)

    def barrier(self):
        sem = pltpu.get_barrier_semaphore()
        peers = [self.partner()] + [self.at(a, s) for a in "xyz" for s in (1, 2, 3)]
        for peer in peers:
            pl.semaphore_signal(sem, inc=1, device_id=peer, device_id_type=MESH)
        pl.semaphore_wait(sem, len(peers))

    def copy(self, src, dst, device):
        k = self.used
        self.used += 1
        c = pltpu.make_async_remote_copy(
            src_ref=src,
            dst_ref=dst,
            send_sem=self.send.at[k],
            recv_sem=self.recv.at[k],
            device_id=device,
            device_id_type=MESH,
        )
        c.start()
        return c


def rows(start, size):
    return pl.ds(pl.multiple_of(start, 8), size)


def exchange(net, axis, src, slots):
    return [net.copy(src, slots.at[d - 1], net.at(axis, d)) for d in (1, 2, 3)]


def wait_all(copies):
    for c in copies:
        c.wait()


def all_reduce_wide(net, part, total, core_in, y_in, x_own, x_in, z_own, z_in):
    other, own = (1 - net.core) * 32, net.core * 32
    net.copy(part.at[rows(other, 32)], core_in, net.partner()).wait()
    core_in[...] += part[rows(own, 32), :]
    copies = [
        net.copy(core_in.at[rows((net.y + d) % 4 * 8, 8)], y_in.at[d - 1], net.at("y", d))
        for d in (1, 2, 3)
    ]
    wait_all(copies)
    x_own[...] = core_in[rows(net.y * 8, 8), :] + y_in[0] + y_in[1] + y_in[2]
    wait_all(exchange(net, "x", x_own, x_in))
    z_own[...] = x_own[...] + x_in[0] + x_in[1] + x_in[2]
    wait_all(exchange(net, "z", z_own, z_in))
    mine = rows(own + net.y * 8, 8)
    total[mine, :] = z_own[...] + z_in[0] + z_in[1] + z_in[2]
    copies = [net.copy(total.at[mine], total.at[mine], net.at("y", d)) for d in (1, 2, 3)]
    wait_all(copies)
    half = rows(own, 32)
    net.copy(total.at[half], total.at[half], net.partner()).wait()


def project(resid, factor, part):
    part[:, 0:D] = dot(resid, factor[...], NT, HI)
    part[:, D:] = jnp.concatenate([dot(resid, resid, NT, HI), jnp.zeros((M, M), F32)], 1)


def precondition(resid, factor, weight, total):
    proj = total[:, 0:D]
    weighted = proj * weight[...]
    precond = resid + dot(weighted, factor[...], NN, HI)
    rho = total[:, D : D + M] + dot(weighted, proj, NT, HI)
    return precond, rho


def gather(net, direc, rowb, colb):
    y, z, x, core = net.y, net.z, net.x, net.core
    for b in (0, 1):
        block = direc[:, b * B : (b + 1) * B].astype(BF16)
        rowb[z, x, b] = block
        colb[y, core, b] = block
    lo, hi = pl.ds(0, 32), pl.ds(32, 32)

    def blk(b, first, second):
        return (((z + second) % 4, (x + first) % 4) if b == 0 else ((z + first) % 4, (x + second) % 4)) + (b,)

    firsts, seconds = ("x", "z"), ("z", "x")
    done = []

    def send(ref, device):
        c = net.copy(ref, ref, device)
        done.append(c)
        return c

    one = {}
    for b in (0, 1):
        ref = rowb.at[blk(b, 0, 0)]
        one[b] = [send(ref, net.at(firsts[b], 1)), send(ref, net.at(firsts[b], -1))]
    ref = colb.at[y, core]
    col_one = [send(ref, net.at("y", 1)), send(ref, net.at("y", -1))]
    col_core = [send(ref, net.partner())]

    two, second = {}, {0: {}, 1: {}}

    def spread(b, first):
        ref = rowb.at[blk(b, first, 0)]
        second[b][first] = [send(ref, net.at(seconds[b], 1)), send(ref, net.at(seconds[b], -1))]

    for b in (0, 1):
        spread(b, 0)
    for b in (0, 1):
        one[b][0].wait_recv()
        before = rowb.at[blk(b, -1, 0)]
        two[b] = [send(before.at[lo], net.at(firsts[b], 1))]
        one[b][1].wait_recv()
        after = rowb.at[blk(b, 1, 0)]
        two[b].append(send(after.at[hi], net.at(firsts[b], -1)))
    col_one[0].wait_recv()
    col_two = [send(colb.at[(y + 3) % 4, core, 0], net.at("y", 1))]
    col_one[1].wait_recv()
    col_two.append(send(colb.at[(y + 1) % 4, core, 1], net.at("y", -1)))
    for b in (0, 1):
        spread(b, -1)
        spread(b, 1)
    for step in (-1, 1):
        col_core.append(send(colb.at[(y + step) % 4, core], net.partner()))
    last = []

    def relay(b, first):
        up, down = second[b][first]
        up.wait_recv()
        ref = rowb.at[blk(b, first, -1)]
        last.append(send(ref.at[lo], net.at(seconds[b], 1)))
        down.wait_recv()
        ref = rowb.at[blk(b, first, 1)]
        last.append(send(ref.at[hi], net.at(seconds[b], -1)))

    for b in (0, 1):
        relay(b, 0)
    for b in (0, 1):
        two[b][0].wait_recv()
        two[b][1].wait_recv()
        spread(b, 2)
    for c in col_two:
        c.wait_recv()
    col_core.append(send(colb.at[(y + 2) % 4, core], net.partner()))
    for first in (-1, 1, 2):
        for b in (0, 1):
            relay(b, first)
    for c in last + col_core:
        c.wait_recv()
    for c in done:
        c.wait_send()


class Ring:
    def __init__(self, net, axis, chunk, via, direct, final):
        self.net, self.axis, self.chunk = net, axis, chunk
        self.via, self.direct, self.final = via, direct, final
        self.done = []

    def send(self, src, dst, step):
        c = self.net.copy(src, dst, self.net.at(self.axis, step))
        self.done.append(c)
        return c

    def start(self):
        chunk = self.chunk
        self.one = [self.send(chunk(2, 0), self.via.at[0], 1), self.send(chunk(2, 1), self.via.at[1], -1)]
        self.straight = [
            self.send(chunk(1, 1), self.direct.at[1], 1),
            self.send(chunk(-1, 0), self.direct.at[0], -1),
        ]

    def forward(self):
        self.two = []
        for half, step in ((0, 1), (1, -1)):
            self.one[half].wait_recv()
            self.via[half] += self.chunk(step, half)[...]
            self.two.append(self.send(self.via.at[half], self.final.at[half], step))

    def result(self, half):
        self.two[half].wait_recv()
        self.straight[1 - half].wait_recv()
        return self.final[half] + self.direct[half]

    def close(self):
        for c in self.done:
            c.wait_send()


def solve(left, right, eye=None):
    table = jnp.concatenate([left, right], 1)
    row_ids = lax.broadcasted_iota(jnp.int32, (M, 2 * M), 0)
    for k in range(M):
        pivot = table[k : k + 1, :] * (1.0 / table[k : k + 1, k : k + 1])
        column = jnp.where(row_ids[:, 0:1] == k, 0.0, table[:, k : k + 1])
        table = jnp.where(row_ids == k, pivot, table - column * pivot)
    return table[:, M:]


def scatter_sums(net, fwd, trans, bufs, beside):
    via_a, dir_a, fin_a, mid, via_b, dir_b, fin_b, core_in, via_y, dir_y, fin_y = bufs
    y, z, x, core = net.y, net.z, net.x, net.core
    half = (pl.ds(0, 32), pl.ds(32, 32))

    def first_chunk(b):
        if b == 0:
            return lambda step, h: fwd.at[:, (x + step) % 4, 0, half[h]]
        return lambda step, h: fwd.at[(z + step) % 4, :, 1, half[h]]

    axes = ("x", "z")
    rings = [Ring(net, axes[b], first_chunk(b), via_a.at[b], dir_a.at[b], fin_a.at[b]) for b in (0, 1)]
    core_copies = {}
    for step in (2, 1, -1, 0):
        to = (y + step) % 4
        core_copies[step] = net.copy(trans.at[to, 1 - core], core_in.at[to], net.partner())
    for r in rings:
        r.start()
    beside[0]()
    ring_y = Ring(net, "y", lambda step, h: core_in.at[(y + step) % 4, h], via_y, dir_y, fin_y)
    for step in (2, 1, -1, 0):
        core_copies[step].wait()
        to = (y + step) % 4
        core_in[to] += trans[to, core]
    ring_y.start()
    beside[1]()
    for r in rings:
        r.forward()
    beside[2]()
    ring_y.forward()
    seconds = []
    for b in (0, 1):
        for h in (0, 1):
            own = first_chunk(b)(0, h)[...]
            mid[b, :, h * 32 : h * 32 + 32, :] = own + rings[b].result(h)
        pos = z if b == 0 else x
        chunk = lambda step, h, b=b, pos=pos: mid.at[b, (pos + step) % 4, half[h]]
        r = Ring(net, axes[1 - b], chunk, via_b.at[b], dir_b.at[b], fin_b.at[b])
        r.start()
        seconds.append(r)
    beside[3]()
    for r in seconds:
        r.forward()
    beside[4]()
    for b in (0, 1):
        ring_y.result(b)
    image = []
    for b in (0, 1):
        column = core_in[y, b] + (fin_y[b] + dir_y[b])
        parts = [seconds[b].chunk(0, h)[...] + seconds[b].result(h) for h in (0, 1)]
        image.append(column + jnp.concatenate(parts, 0))
    for r in rings + seconds + [ring_y]:
        r.close()
    return jnp.concatenate(image, 1)


def split3(a):
    high = a.astype(BF16)
    rest = a - high.astype(F32)
    middle = rest.astype(BF16)
    low = (rest - middle.astype(F32)).astype(BF16)
    return jnp.concatenate([high, middle, low], 0)


class Gram:
    def __init__(self, net, fwd, rowb, direc, self_term, own, slots):
        self.net, self.fwd, self.rowb = net, fwd, rowb
        self.direc, self.self_term, self.own, self.slots = direc, self_term, own, slots

    def local(self):
        def step(k, acc):
            q, b = k // 2, k % 2
            return acc + dot(self.rowb[q // 4, q % 4, b], split3(self.fwd[q // 4, q % 4, b]), NT)

        thirds = lax.fori_loop(0, 32, step, jnp.zeros((M, 3 * M), F32))
        h = thirds[:, 0:M] + thirds[:, M : 2 * M] + thirds[:, 2 * M :]
        direc = self.direc[...]
        g = h + h.T + dot(direc * self.self_term[...], direc, NT, HI)
        self.own[0] = jnp.concatenate([g[0:32], g[32:64]], 1)
        self.copies = [self.net.copy(self.own.at[0], self.slots.at[0, 0], self.net.partner())]

    def stage(self, k):
        wait_all(self.copies)
        got = self.slots[k, 0] if k == 0 else self.slots[k, 0] + self.slots[k, 1] + self.slots[k, 2]
        self.own[k + 1] = self.own[k] + got
        if k < 3:
            self.copies = exchange(self.net, "yxz"[k], self.own.at[k + 1], self.slots.at[k + 1])

    def total(self):
        g = self.own[4]
        return jnp.concatenate([g[:, 0:M], g[:, M:]], 0)


def first_kernel(rhs, factor, weight, direc, rho, rowb, colb, part, total, *rest):
    *bufs, send, recv = rest
    net = Net(send, recv)
    net.barrier()
    resid = rhs[...]
    project(resid, factor, part)
    all_reduce_wide(net, part, total, *bufs)
    precond, rho_value = precondition(resid, factor, weight, total)
    direc[...] = precond
    rho[...] = rho_value
    gather(net, precond, rowb, colb)


def step_kernel(last, *refs):
    if last:
        (fwd, trans, row_in, direc, resid, sol, self_term, rho, sol_out, resid_out, own, slots, *rest) = refs
        bufs, (alpha_ref, send, recv) = rest[:11], rest[11:]
    else:
        (fwd, trans, row_in, direc, resid, self_term, rho, factor, weight) = refs[:9]
        (sol_out, resid_out, direc_out, rho_out, rowb, colb, own, slots, *rest) = refs[9:]
        bufs, (alpha_ref, beta_ref, part, total, *wide, send, recv) = rest[:11], rest[11:]
    net = Net(send, recv)
    gram = Gram(net, fwd, row_in, direc, self_term, own, slots)
    net.barrier()

    def local():
        gram.local()

    def after_core():
        gram.stage(0)

    def invert():
        gram.stage(1)
        if not last:
            eye = lax.broadcasted_iota(jnp.int32, (M, M), 0) == lax.broadcasted_iota(jnp.int32, (M, M), 1)
            beta_ref[...] = solve(rho[...], eye.astype(F32))

    def across():
        gram.stage(2)

    def alpha():
        gram.stage(3)
        g = gram.total()
        alpha_ref[...] = solve((g + g.T) * 0.5, rho[...])

    image = self_term[...] * direc[...] + scatter_sums(net, fwd, trans, bufs, [local, after_core, invert, across, alpha])
    step = dot(alpha_ref[...], direc[...], TN, HI)
    sol_out[...] = sol[...] + step if last else step
    residual = resid[...] - dot(alpha_ref[...], image, TN, HI)
    resid_out[...] = residual
    if not last:
        project(residual, factor, part)
        all_reduce_wide(net, part, total, *wide)
        precond, rho_value = precondition(residual, factor, weight, total)
        rho_out[...] = rho_value
        beta = dot(beta_ref[...], rho_value, NN, HI)
        fresh = precond + dot(beta, direc[...], TN, HI)
        direc_out[...] = fresh
        gather(net, fresh, rowb, colb)


def operate_kernel(count, near_rows, near_cols, far_rows, far_cols, rowb, colb, left, right, tiles, fwd, trans, held, sem):
    n = count[0]
    chunks = (n + GROUP - 1) // GROUP
    depth = held.shape[0]

    def load(k):
        return pltpu.make_async_copy(
            tiles.at[pl.ds(k * GROUP, GROUP)], held.at[lax.rem(k, depth)], sem.at[lax.rem(k, depth)]
        )

    for k in range(depth - 1):

        @pl.when(k < chunks)
        def _():
            load(k).start()

    fwd[...] = jnp.zeros_like(fwd)
    trans[...] = jnp.zeros_like(trans)

    def far(k, carry):
        out = []
        for g in range(GROUP):
            p = k * GROUP + g
            r, c = far_rows[p], far_cols[p]
            half_f = dot(colb[c], right[p], NT).astype(BF16)
            half_t = dot(rowb[r], left[p], NT).astype(BF16)
            out.append((r, c, dot(half_f, left[p]), dot(half_t, right[p])))
        for r, c, f, t in out:
            fwd[r] += f
            trans[c] += t
        return carry

    lax.fori_loop(0, left.shape[0] // GROUP, far, 0)

    def near(k, carry):
        load(k).wait()

        @pl.when(k + depth - 1 < chunks)
        def _():
            load(k + depth - 1).start()

        slot = lax.rem(k, depth)
        for g0 in range(0, GROUP, 4):
            out = []
            for g in range(g0, g0 + 4):
                s = k * GROUP + g
                r, c = near_rows[s], near_cols[s]
                tile = held[slot, g]
                valid = s < n
                f = jnp.where(valid, dot(colb[c], tile, NT), 0.0)
                t = jnp.where(valid, dot(rowb[r], tile), 0.0)
                out.append((r, c, f, t))
            for r, c, f, t in out:
                fwd[r] += f
                trans[c] += t
        return carry

    lax.fori_loop(0, chunks, near, 0)


def shape(*dims, dtype=F32):
    return jax.ShapeDtypeStruct(dims, dtype)


def wide_scratch():
    v = pltpu.VMEM
    return [
        v((M, WIDE), F32),
        v((M, WIDE), F32),
        v((32, WIDE), F32),
        v((3, 8, WIDE), F32),
        v((8, WIDE), F32),
        v((3, 8, WIDE), F32),
        v((8, WIDE), F32),
        v((3, 8, WIDE), F32),
    ]


def scatter_scratch():
    v = pltpu.VMEM
    return (
        [v((5, 32, 128), F32), v((4, 3, 32, 128), F32)]
        + [v((2, 2, 4, 32, B), F32)] * 3
        + [v((2, 4, M, B), F32)]
        + [v((2, 2, 32, B), F32)] * 3
        + [v((4, 2, M, B), F32)]
        + [v((2, M, B), F32)] * 3
    )


def sems(n):
    return [pltpu.SemaphoreType.DMA((n,)), pltpu.SemaphoreType.DMA((n,))]


def params(collective):
    return pltpu.CompilerParams(
        collective_id=collective, has_side_effects=True, vmem_limit_bytes=60 * 1024 * 1024
    )


def local(
    rhs, self_term, near_tiles, near_rows, near_cols, near_counts, far_left, far_right, far_rows, far_cols, nys_factor, nys_weight
):
    n_col = lax.axis_size("col")
    count = lax.dynamic_slice(near_counts, (lax.axis_index("row") * n_col + lax.axis_index("col"),), (1,))
    left, right = jnp.swapaxes(far_left, 1, 2), jnp.swapaxes(far_right, 1, 2)
    weight = nys_weight.reshape(1, -1)
    self_row = self_term.reshape(1, -1)
    row_shape = shape(4, 4, 2, M, B, dtype=BF16)
    col_shape = shape(4, 2, 2, M, B, dtype=BF16)
    n_wide = 1 + 3 + 3 + 3 + 3 + 1
    n_gather = 4 + 2 + 4 + 2 + 4 + 2 * 4 * 2 + 16
    n_scatter = 6 * 5 + 4 + 10

    direc, rho, rowb, colb = pl.pallas_call(
        first_kernel,
        out_shape=(shape(M, D), shape(M, M), row_shape, col_shape),
        in_specs=[VMEM] * 3,
        out_specs=(VMEM,) * 4,
        scratch_shapes=wide_scratch() + sems(n_wide + n_gather),
        compiler_params=params(0),
        name="first",
    )(rhs, nys_factor, weight)

    def operate(rowb, colb):
        fwd, trans = pl.pallas_call(
            operate_kernel,
            out_shape=(shape(32, M, B), shape(16, M, B)),
            in_specs=[SMEM] * 5 + [VMEM] * 4 + [ANY],
            out_specs=(VMEM, VMEM),
            scratch_shapes=[pltpu.VMEM((4, GROUP, B, B), BF16), pltpu.SemaphoreType.DMA((4,))],
            compiler_params=pltpu.CompilerParams(vmem_limit_bytes=60 * 1024 * 1024),
            name="operate",
        )(count, near_rows, near_cols, far_rows, far_cols, rowb.reshape(32, M, B), colb.reshape(16, M, B), left, right, near_tiles)
        return fwd.reshape(4, 4, 2, M, B), trans.reshape(4, 2, 2, M, B)

    fwd, trans = operate(rowb, colb)
    square = pltpu.VMEM((M, M), F32)
    sol, residual, direc, rho_next, rowb, colb = pl.pallas_call(
        functools.partial(step_kernel, False),
        out_shape=(shape(M, D), shape(M, D), shape(M, D), shape(M, M), row_shape, col_shape),
        in_specs=[VMEM] * 9,
        out_specs=(VMEM,) * 6,
        scratch_shapes=scatter_scratch() + [square, square] + wide_scratch() + sems(n_wide + n_gather + n_scatter),
        compiler_params=params(1),
        name="middle",
    )(fwd, trans, rowb, direc, rhs, self_row, rho, nys_factor, weight)
    fwd, trans = operate(rowb, colb)
    return pl.pallas_call(
        functools.partial(step_kernel, True),
        out_shape=(shape(M, D), shape(M, D)),
        in_specs=[VMEM] * 8,
        out_specs=(VMEM,) * 2,
        scratch_shapes=scatter_scratch() + [square] + sems(n_scatter),
        compiler_params=params(2),
        name="last",
    )(fwd, trans, rowb, direc, residual, sol, self_row, rho_next)


def solution(mesh):
    split = ("row", "col")
    in_specs = (
        P(None, split),
        P(split),
        P(split, None, None),
        P(split),
        P(split),
        P(),
        P(split, None, None),
        P(split, None, None),
        P(split),
        P(split),
        P(None, split),
        P(),
    )
    out_specs = (P(None, split), P(None, split))
    return jax.shard_map(local, mesh=mesh, in_specs=in_specs, out_specs=out_specs, check_vma=False)
```

```python
import functools

import jax
import jax.numpy as jnp
from jax import lax
from jax.experimental import pallas as pl
from jax.experimental.pallas import tpu as pltpu
from jax.sharding import PartitionSpec as P

MESH = pl.DeviceIdType.MESH
HI = lax.Precision.HIGHEST
F32 = jnp.float32
BF16 = jnp.bfloat16
VMEM = pl.BlockSpec(memory_space=pltpu.VMEM)
SMEM = pl.BlockSpec(memory_space=pltpu.SMEM)
HBM = pl.BlockSpec(memory_space=pltpu.HBM)
NT = (((1,), (1,)), ((), ()))
NN = (((1,), (0,)), ((), ()))
TN = (((0,), (0,)), ((), ()))
M = 64
B = 256
D = 512
CHUNK = 384
GROUP = 8
VMEM_LIMIT = 16 * 1024 * 1024


def dot(a, b, dims=NN, precision=None):
    return lax.dot_general(a, b, dims, precision=precision, preferred_element_type=F32)


class Net:
    def __init__(self, send, recv):
        self.send, self.recv, self.used = send, recv, 0
        self.i, self.j = lax.axis_index("row"), lax.axis_index("col")
        self.y, self.core = self.i // 2, self.i % 2
        self.z, self.x = self.j // 4, self.j % 4

    def partner(self):
        return (self.y * 2 + 1 - self.core, self.j)

    def at(self, axis, step):
        if axis == "y":
            return ((self.y + step) % 4 * 2 + self.core, self.j)
        if axis == "z":
            return (self.i, (self.z + step) % 4 * 4 + self.x)
        return (self.i, self.z * 4 + (self.x + step) % 4)

    def plane(self):
        steps = [(dz, dx) for dz in (0, 1, 3, 2) for dx in (0, 1, 3, 2)][1:]
        return [(self.i, (self.z + dz) % 4 * 4 + (self.x + dx) % 4) for dz, dx in steps]

    def column(self):
        return [((self.i + d) % 8, self.j) for d in range(1, 8)]

    def barrier(self):
        sem = pltpu.get_barrier_semaphore()
        peers = self.column() + self.plane()
        for peer in peers:
            pl.semaphore_signal(sem, inc=1, device_id=peer, device_id_type=MESH)
        pl.semaphore_wait(sem, len(peers))

    def copy(self, src, dst, device):
        k = self.used
        self.used += 1
        c = pltpu.make_async_remote_copy(
            src_ref=src,
            dst_ref=dst,
            send_sem=self.send.at[k],
            recv_sem=self.recv.at[k],
            device_id=device,
            device_id_type=MESH,
        )
        c.start()
        return c


def rows(start, size):
    return pl.ds(pl.multiple_of(start, 8), size)


def exchange(net, axis, src, slots):
    return [net.copy(src, slots.at[d - 1], net.at(axis, d)) for d in (1, 2, 3)]


def wait_all(copies):
    for c in copies:
        c.wait()


def all_reduce_wide(net, part, total, plane_in, row_own, row_in):
    me = net.j
    wait_all([net.copy(part.at[p[1]], plane_in.at[k], p) for k, p in enumerate(net.plane())])
    row_own[...] = part[me] + jnp.sum(plane_in[...], 0)
    wait_all([net.copy(row_own, row_in.at[k], p) for k, p in enumerate(net.column())])
    total[me] = row_own[...] + jnp.sum(row_in[...], 0)
    wait_all([net.copy(total.at[me], total.at[me], p) for p in net.plane()])


def project(resid, factor, part):
    proj = dot(resid, factor[...], NT, HI)
    inner = dot(resid, resid, NT, HI)
    wide = jnp.concatenate([proj, inner, jnp.zeros((M, 2 * CHUNK - D - M), F32)], 1)
    for q in range(16):
        part[q] = wide[q // 2 * 8 : q // 2 * 8 + 8, q % 2 * CHUNK : q % 2 * CHUNK + CHUNK]


def precondition(resid, factor, weight, total):
    lines = [jnp.concatenate([total[2 * q], total[2 * q + 1]], 1) for q in range(8)]
    wide = jnp.concatenate(lines, 0)
    proj = wide[:, 0:D]
    weighted = proj * weight[...]
    precond = resid + dot(weighted, factor[...], NN, HI)
    rho = wide[:, D : D + M] + dot(weighted, proj, NT, HI)
    return precond, rho


def gather(net, direc, rowb, colb):
    y, z, x, core = net.y, net.z, net.x, net.core
    for b in (0, 1):
        block = direc[:, b * B : (b + 1) * B].astype(BF16)
        rowb[z, x, b] = block
        colb[y, core, b] = block
    lo, hi = pl.ds(0, 32), pl.ds(32, 32)

    def blk(b, first, second):
        return (((z + second) % 4, (x + first) % 4) if b == 0 else ((z + first) % 4, (x + second) % 4)) + (b,)

    firsts, seconds = ("x", "z"), ("z", "x")
    done = []

    def send(ref, device):
        c = net.copy(ref, ref, device)
        done.append(c)
        return c

    one = {}
    for b in (0, 1):
        ref = rowb.at[blk(b, 0, 0)]
        one[b] = [send(ref, net.at(firsts[b], 1)), send(ref, net.at(firsts[b], -1))]
    ref = colb.at[y, core]
    col_one = [send(ref, net.at("y", 1)), send(ref, net.at("y", -1))]
    col_core = [send(ref, net.partner())]

    two, second = {}, {0: {}, 1: {}}

    def spread(b, first):
        ref = rowb.at[blk(b, first, 0)]
        second[b][first] = [send(ref, net.at(seconds[b], 1)), send(ref, net.at(seconds[b], -1))]

    for b in (0, 1):
        spread(b, 0)
    for b in (0, 1):
        one[b][0].wait_recv()
        before = rowb.at[blk(b, -1, 0)]
        two[b] = [send(before.at[lo], net.at(firsts[b], 1))]
        one[b][1].wait_recv()
        after = rowb.at[blk(b, 1, 0)]
        two[b].append(send(after.at[hi], net.at(firsts[b], -1)))
    col_one[0].wait_recv()
    col_two = [send(colb.at[(y + 3) % 4, core, 0], net.at("y", 1))]
    col_one[1].wait_recv()
    col_two.append(send(colb.at[(y + 1) % 4, core, 1], net.at("y", -1)))
    for b in (0, 1):
        spread(b, -1)
        spread(b, 1)
    for step in (-1, 1):
        col_core.append(send(colb.at[(y + step) % 4, core], net.partner()))
    last = []

    def relay(b, first):
        up, down = second[b][first]
        up.wait_recv()
        ref = rowb.at[blk(b, first, -1)]
        last.append(send(ref.at[lo], net.at(seconds[b], 1)))
        down.wait_recv()
        ref = rowb.at[blk(b, first, 1)]
        last.append(send(ref.at[hi], net.at(seconds[b], -1)))

    for b in (0, 1):
        relay(b, 0)
    for b in (0, 1):
        two[b][0].wait_recv()
        two[b][1].wait_recv()
        spread(b, 2)
    for c in col_two:
        c.wait_recv()
    col_core.append(send(colb.at[(y + 2) % 4, core], net.partner()))
    for first in (-1, 1, 2):
        for b in (0, 1):
            relay(b, first)
    for c in last + col_core:
        c.wait_recv()
    for c in done:
        c.wait_send()


class Ring:
    def __init__(self, net, axis, chunk, via, direct, final):
        self.net, self.axis, self.chunk = net, axis, chunk
        self.via, self.direct, self.final = via, direct, final
        self.done = []

    def send(self, src, dst, step):
        c = self.net.copy(src, dst, self.net.at(self.axis, step))
        self.done.append(c)
        return c

    def start(self):
        chunk = self.chunk
        self.one = [self.send(chunk(2, 0), self.via.at[0], 1), self.send(chunk(2, 1), self.via.at[1], -1)]
        self.straight = [
            self.send(chunk(1, 1), self.direct.at[1], 1),
            self.send(chunk(-1, 0), self.direct.at[0], -1),
        ]

    def forward(self):
        self.two = []
        for half, step in ((0, 1), (1, -1)):
            self.one[half].wait_recv()
            self.via[half] += self.chunk(step, half)[...]
            self.two.append(self.send(self.via.at[half], self.final.at[half], step))

    def result(self, half):
        self.two[half].wait_recv()
        self.straight[1 - half].wait_recv()
        return self.final[half] + self.direct[half]

    def close(self):
        for c in self.done:
            c.wait_send()


def solve(left, right, eye=None):
    table = jnp.concatenate([left, right], 1)
    row_ids = lax.broadcasted_iota(jnp.int32, (M, 2 * M), 0)
    for k in range(M):
        pivot = table[k : k + 1, :] * (1.0 / table[k : k + 1, k : k + 1])
        column = jnp.where(row_ids[:, 0:1] == k, 0.0, table[:, k : k + 1])
        table = jnp.where(row_ids == k, pivot, table - column * pivot)
    return table[:, M:]


def scatter_sums(net, fwd, trans, bufs, beside):
    via_a, dir_a, fin_a, mid, via_b, dir_b, fin_b, core_in, via_y, dir_y, fin_y = bufs
    y, z, x, core = net.y, net.z, net.x, net.core
    half = (pl.ds(0, 32), pl.ds(32, 32))

    def first_chunk(b):
        if b == 0:
            return lambda step, h: fwd.at[:, (x + step) % 4, 0, half[h]]
        return lambda step, h: fwd.at[(z + step) % 4, :, 1, half[h]]

    axes = ("x", "z")
    rings = [Ring(net, axes[b], first_chunk(b), via_a.at[b], dir_a.at[b], fin_a.at[b]) for b in (0, 1)]
    core_copies = {}
    for step in (2, 1, -1, 0):
        to = (y + step) % 4
        core_copies[step] = net.copy(trans.at[to, 1 - core], core_in.at[to], net.partner())
    for r in rings:
        r.start()
    beside[0]()
    ring_y = Ring(net, "y", lambda step, h: core_in.at[(y + step) % 4, h], via_y, dir_y, fin_y)
    for step in (2, 1, -1, 0):
        core_copies[step].wait()
        to = (y + step) % 4
        core_in[to] += trans[to, core]
    ring_y.start()
    beside[1]()
    for r in rings:
        r.forward()
    beside[2]()
    ring_y.forward()
    seconds = []
    for b in (0, 1):
        for h in (0, 1):
            own = first_chunk(b)(0, h)[...]
            mid[b, :, h * 32 : h * 32 + 32, :] = own + rings[b].result(h)
        pos = z if b == 0 else x
        chunk = lambda step, h, b=b, pos=pos: mid.at[b, (pos + step) % 4, half[h]]
        r = Ring(net, axes[1 - b], chunk, via_b.at[b], dir_b.at[b], fin_b.at[b])
        r.start()
        seconds.append(r)
    beside[3]()
    for r in seconds:
        r.forward()
    beside[4]()
    for b in (0, 1):
        ring_y.result(b)
    image = []
    for b in (0, 1):
        column = core_in[y, b] + (fin_y[b] + dir_y[b])
        parts = [seconds[b].chunk(0, h)[...] + seconds[b].result(h) for h in (0, 1)]
        image.append(column + jnp.concatenate(parts, 0))
    for r in rings + seconds + [ring_y]:
        r.close()
    return jnp.concatenate(image, 1)


def split3(a):
    high = a.astype(BF16)
    rest = a - high.astype(F32)
    middle = rest.astype(BF16)
    low = (rest - middle.astype(F32)).astype(BF16)
    return jnp.concatenate([high, middle, low], 0)


class Gram:
    def __init__(self, net, fwd, rowb, direc, self_term, own, slots):
        self.net, self.fwd, self.rowb = net, fwd, rowb
        self.direc, self.self_term, self.own, self.slots = direc, self_term, own, slots

    def local(self):
        def step(k, acc):
            for t in range(8):
                q = k * 4 + t // 2
                at = (q // 4, q % 4, t % 2)
                acc = acc + dot(self.rowb[at], split3(self.fwd[at]), NT)
            return acc

        thirds = lax.fori_loop(0, 4, step, jnp.zeros((M, 3 * M), F32))
        h = thirds[:, 0:M] + thirds[:, M : 2 * M] + thirds[:, 2 * M :]
        direc = self.direc[...]
        g = h + h.T + dot(direc * self.self_term[...], direc, NT, HI)
        self.own[0] = jnp.concatenate([g[0:32], g[32:64]], 1)
        self.copies = [self.net.copy(self.own.at[0], self.slots.at[0, 0], self.net.partner())]

    def stage(self, k):
        wait_all(self.copies)
        got = self.slots[k, 0] if k == 0 else self.slots[k, 0] + self.slots[k, 1] + self.slots[k, 2]
        self.own[k + 1] = self.own[k] + got
        if k < 3:
            self.copies = exchange(self.net, "yxz"[k], self.own.at[k + 1], self.slots.at[k + 1])

    def total(self):
        g = self.own[4]
        return jnp.concatenate([g[:, 0:M], g[:, M:]], 0)


def first_kernel(*refs):
    sources, (direc, rho, rowb, colb), kept = refs[:6], refs[6:10], refs[10:16]
    part, total, *bufs, send, recv, local_sem = refs[16:]
    rhs, factor, weight = kept[:3]
    copies = [pltpu.make_async_copy(a, b, local_sem.at[k]) for k, (a, b) in enumerate(zip(sources, kept))]
    for c in copies:
        c.start()
    net = Net(send, recv)
    net.barrier()
    for c in copies[:3]:
        c.wait()
    resid = rhs[...]
    project(resid, factor, part)
    all_reduce_wide(net, part, total, *bufs)
    precond, rho_value = precondition(resid, factor, weight, total)
    direc[...] = precond
    rho[...] = rho_value
    gather(net, precond, rowb, colb)
    for c in copies[3:]:
        c.wait()


def step_kernel(last, *refs):
    if last:
        (fwd, trans, row_in, direc, resid, sol, self_term, rho, sol_out, resid_out, own, slots, *rest) = refs
        bufs, (alpha_ref, send, recv) = rest[:11], rest[11:]
    else:
        (fwd, trans, row_in, direc, resid, self_term, rho, factor, weight) = refs[:9]
        (sol_out, resid_out, direc_out, rho_out, rowb, colb, own, slots, *rest) = refs[9:]
        bufs, (alpha_ref, beta_ref, part, total, *wide, send, recv) = rest[:11], rest[11:]
    net = Net(send, recv)
    gram = Gram(net, fwd, row_in, direc, self_term, own, slots)
    net.barrier()

    def local():
        gram.local()

    def after_core():
        gram.stage(0)

    def invert():
        gram.stage(1)
        if not last:
            eye = lax.broadcasted_iota(jnp.int32, (M, M), 0) == lax.broadcasted_iota(jnp.int32, (M, M), 1)
            beta_ref[...] = solve(rho[...], eye.astype(F32))

    def across():
        gram.stage(2)

    def alpha():
        gram.stage(3)
        g = gram.total()
        alpha_ref[...] = solve((g + g.T) * 0.5, rho[...])

    image = self_term[...] * direc[...] + scatter_sums(net, fwd, trans, bufs, [local, after_core, invert, across, alpha])
    step = dot(alpha_ref[...], direc[...], TN, HI)
    sol_out[...] = sol[...] + step if last else step
    residual = resid[...] - dot(alpha_ref[...], image, TN, HI)
    resid_out[...] = residual
    if not last:
        project(residual, factor, part)
        all_reduce_wide(net, part, total, *wide)
        precond, rho_value = precondition(residual, factor, weight, total)
        rho_out[...] = rho_value
        beta = dot(beta_ref[...], rho_value, NN, HI)
        fresh = precond + dot(beta, direc[...], TN, HI)
        direc_out[...] = fresh
        gather(net, fresh, rowb, colb)


def operate_kernel(*refs):
    sources, (rowb, colb, left, right, tiles, fwd, trans, half_f, half_t), tables, sem = refs[:5], refs[5:14], refs[14:19], refs[19]
    copies = [pltpu.make_async_copy(a, b, sem.at[k]) for k, (a, b) in enumerate(zip(sources, tables))]
    for c in copies:
        c.start()
    fwd[...] = jnp.zeros_like(fwd)
    trans[...] = jnp.zeros_like(trans)
    for c in copies:
        c.wait()
    counts, near_rows, near_cols, far_rows, far_cols = tables
    n = counts[lax.axis_index("row") * lax.axis_size("col") + lax.axis_index("col")]

    def far_halves(k, carry):
        for g in range(16):
            p = k * 16 + g
            half_f[p] = dot(colb[far_cols[p]], right[p], NT).astype(BF16)
            half_t[p] = dot(rowb[far_rows[p]], left[p], NT).astype(BF16)
        return carry

    def far(k, carry):
        out = []
        for g in range(8):
            p = k * 8 + g
            out.append((far_rows[p], far_cols[p], dot(half_f[p], left[p]), dot(half_t[p], right[p])))
        for r, c, f, t in out:
            fwd[r] += f
            trans[c] += t
        return carry

    lax.fori_loop(0, left.shape[0] // 16, far_halves, 0)
    lax.fori_loop(0, left.shape[0] // 8, far, 0)

    def near(k, carry):
        out = []
        for g in range(GROUP):
            s = k * GROUP + g
            r, c = near_rows[s], near_cols[s]
            tile = tiles[s]
            valid = s < n
            f = jnp.where(valid, dot(colb[c], tile, NT), 0.0)
            t = jnp.where(valid, dot(rowb[r], tile), 0.0)
            out.append((r, c, f, t))
        for r, c, f, t in out:
            fwd[r] += f
            trans[c] += t
        return carry

    lax.fori_loop(0, (n + GROUP - 1) // GROUP, near, 0)


def shape(*dims, dtype=F32):
    return jax.ShapeDtypeStruct(dims, dtype)


def wide_scratch():
    v = pltpu.VMEM
    return [
        v((16, 8, CHUNK), F32),
        v((16, 8, CHUNK), F32),
        v((15, 8, CHUNK), F32),
        v((8, CHUNK), F32),
        v((7, 8, CHUNK), F32),
    ]


def scatter_scratch():
    v = pltpu.VMEM
    return (
        [v((5, 32, 128), F32), v((4, 3, 32, 128), F32)]
        + [v((2, 2, 4, 32, B), F32)] * 3
        + [v((2, 4, M, B), F32)]
        + [v((2, 2, 32, B), F32)] * 3
        + [v((4, 2, M, B), F32)]
        + [v((2, M, B), F32)] * 3
    )


def sems(n):
    return [pltpu.SemaphoreType.DMA((n,)), pltpu.SemaphoreType.DMA((n,))]


def params(collective):
    return pltpu.CompilerParams(
        collective_id=collective, has_side_effects=True, vmem_limit_bytes=VMEM_LIMIT
    )


def local(
    rhs, self_term, near_tiles, near_rows, near_cols, near_counts, far_left, far_right, far_rows, far_cols, nys_factor, nys_weight
):
    left, right = jnp.swapaxes(far_left, 1, 2), jnp.swapaxes(far_right, 1, 2)
    weight = nys_weight.reshape(1, -1)
    self_row = self_term.reshape(1, -1)
    row_shape = shape(4, 4, 2, M, B, dtype=BF16)
    col_shape = shape(4, 2, 2, M, B, dtype=BF16)
    n_wide = 15 + 7 + 15
    n_gather = 4 + 2 + 4 + 2 + 4 + 2 * 4 * 2 + 16
    n_scatter = 6 * 5 + 4 + 10

    sources = (rhs, nys_factor, weight, near_tiles, left, right)
    direc, rho, rowb, colb, resid, factor, weight, tiles, left, right = pl.pallas_call(
        first_kernel,
        out_shape=(shape(M, D), shape(M, M), row_shape, col_shape) + tuple(shape(*a.shape, dtype=a.dtype) for a in sources),
        in_specs=[HBM] * 6,
        out_specs=(VMEM,) * 10,
        scratch_shapes=wide_scratch() + sems(n_wide + n_gather) + [pltpu.SemaphoreType.DMA((6,))],
        compiler_params=params(0),
        name="first",
    )(*[pltpu.with_memory_space_constraint(a, pltpu.HBM) for a in sources])
    tables = (near_counts, near_rows, near_cols, far_rows, far_cols)

    def operate(rowb, colb):
        fwd, trans = pl.pallas_call(
            operate_kernel,
            out_shape=(shape(32, M, B), shape(16, M, B)),
            in_specs=[HBM] * 5 + [VMEM] * 5,
            out_specs=(VMEM, VMEM),
            scratch_shapes=[pltpu.VMEM((far_left.shape[0], M, far_left.shape[2]), BF16)] * 2
            + [pltpu.SMEM(t.shape, jnp.int32) for t in tables]
            + [pltpu.SemaphoreType.DMA((5,))],
            compiler_params=pltpu.CompilerParams(vmem_limit_bytes=VMEM_LIMIT),
            name="operate",
        )(*tables, rowb.reshape(32, M, B), colb.reshape(16, M, B), left, right, tiles)
        return fwd.reshape(4, 4, 2, M, B), trans.reshape(4, 2, 2, M, B)

    fwd, trans = operate(rowb, colb)
    square = pltpu.VMEM((M, M), F32)
    sol, residual, direc, rho_next, rowb, colb = pl.pallas_call(
        functools.partial(step_kernel, False),
        out_shape=(shape(M, D), shape(M, D), shape(M, D), shape(M, M), row_shape, col_shape),
        in_specs=[VMEM] * 9,
        out_specs=(VMEM,) * 6,
        scratch_shapes=scatter_scratch() + [square, square] + wide_scratch() + sems(n_wide + n_gather + n_scatter),
        compiler_params=params(1),
        name="middle",
    )(fwd, trans, rowb, direc, resid, self_row, rho, factor, weight)
    fwd, trans = operate(rowb, colb)
    return pl.pallas_call(
        functools.partial(step_kernel, True),
        out_shape=(shape(M, D), shape(M, D)),
        in_specs=[VMEM] * 8,
        out_specs=(VMEM,) * 2,
        scratch_shapes=scatter_scratch() + [square] + sems(n_scatter),
        compiler_params=params(2),
        name="last",
    )(fwd, trans, rowb, direc, residual, sol, self_row, rho_next)


def solution(mesh):
    split = ("row", "col")
    in_specs = (
        P(None, split),
        P(split),
        P(split, None, None),
        P(split),
        P(split),
        P(),
        P(split, None, None),
        P(split, None, None),
        P(split),
        P(split),
        P(None, split),
        P(),
    )
    out_specs = (P(None, split), P(None, split))
    return jax.shard_map(local, mesh=mesh, in_specs=in_specs, out_specs=out_specs, check_vma=False)
```

```python
import jax
import jax.numpy as jnp
from jax import lax
from jax.experimental import pallas as pl
from jax.experimental.pallas import tpu as pltpu
from jax.sharding import PartitionSpec as P

MESH = pl.DeviceIdType.MESH
HI = lax.Precision.HIGHEST
F32 = jnp.float32
BF16 = jnp.bfloat16
VMEM = pl.BlockSpec(memory_space=pltpu.VMEM)
SMEM = pl.BlockSpec(memory_space=pltpu.SMEM)
HBM = pl.BlockSpec(memory_space=pltpu.HBM)
NT = (((1,), (1,)), ((), ()))
NN = (((1,), (0,)), ((), ()))
TN = (((0,), (0,)), ((), ()))
M = 64
B = 256
D = 512
CHUNK = 384
GROUP = 16
VMEM_LIMIT = 16 * 1024 * 1024


def dot(a, b, dims=NN, precision=None):
    return lax.dot_general(a, b, dims, precision=precision, preferred_element_type=F32)


class Net:
    def __init__(self, send, recv):
        self.send, self.recv, self.used = send, recv, 0
        self.i, self.j = lax.axis_index("row"), lax.axis_index("col")
        self.y, self.core = self.i // 2, self.i % 2
        self.z, self.x = self.j // 4, self.j % 4

    def partner(self):
        return (self.y * 2 + 1 - self.core, self.j)

    def at(self, axis, step):
        if axis == "y":
            return ((self.y + step) % 4 * 2 + self.core, self.j)
        if axis == "z":
            return (self.i, (self.z + step) % 4 * 4 + self.x)
        return (self.i, self.z * 4 + (self.x + step) % 4)

    def plane(self):
        steps = [(dz, dx) for dz in (2, 1, 3, 0) for dx in (2, 1, 3, 0)][:-1]
        steps.sort(key=lambda s: -sum(min(d, 4 - d) for d in s))
        return [(self.i, (self.z + dz) % 4 * 4 + (self.x + dx) % 4) for dz, dx in steps]

    def column(self):
        others = [((self.y + d) % 4 * 2 + (self.core + c) % 2, self.j) for d in (2, 1, 3) for c in (0, 1)]
        return others + [self.partner()]

    def greet(self):
        peers = self.plane() + self.column()
        for peer in peers:
            pl.semaphore_signal(pltpu.get_barrier_semaphore(), inc=1, device_id=peer, device_id_type=MESH)

    def meet(self):
        pl.semaphore_wait(pltpu.get_barrier_semaphore(), 15 + 7)

    def copy(self, src, dst, device):
        k = self.used
        self.used += 1
        c = pltpu.make_async_remote_copy(
            src_ref=src,
            dst_ref=dst,
            send_sem=self.send.at[k],
            recv_sem=self.recv.at[k],
            device_id=device,
            device_id_type=MESH,
        )
        c.start()
        return c


def rows(start, size):
    return pl.ds(pl.multiple_of(start, 8), size)


def exchange(net, axis, src, slots):
    return [net.copy(src, slots.at[d - 1], net.at(axis, d)) for d in (2, 1, 3)]


def wait_all(copies):
    for c in copies:
        c.wait()


def all_reduce_wide(net, part, total, plane_in, row_own, row_in, beside=()):
    me = net.j
    copies = [net.copy(part.at[p[1]], plane_in.at[k], p) for k, p in enumerate(net.plane())]
    for step in beside[:1]:
        step()
    wait_all(copies)
    row_own[...] = part[me] + jnp.sum(plane_in[...], 0)
    copies = [net.copy(row_own, row_in.at[k], p) for k, p in enumerate(net.column())]
    for step in beside[1:2]:
        step()
    wait_all(copies)
    total[me] = row_own[...] + jnp.sum(row_in[...], 0)
    copies = [net.copy(total.at[me], total.at[me], p) for p in net.plane()]
    for step in beside[2:]:
        step()
    wait_all(copies)


def project(a, factor, part, others):
    pieces = [dot(a, factor[...], NT, HI)] + [dot(a, o, NT, HI) for o in others]
    used = D + M * len(others)
    wide = jnp.concatenate(pieces + [jnp.zeros((M, 2 * CHUNK - used), F32)], 1)
    for q in range(16):
        part[q] = wide[q // 2 * 8 : q // 2 * 8 + 8, q % 2 * CHUNK : q % 2 * CHUNK + CHUNK]


def assemble(total):
    return jnp.concatenate([jnp.concatenate([total[2 * q], total[2 * q + 1]], 1) for q in range(8)], 0)


def precondition(resid, proj, inner, factor, weight):
    weighted = proj * weight[...]
    precond = resid + dot(weighted, factor[...], NN, HI)
    return precond, inner + dot(weighted, proj, NT, HI)


def gather(net, direc, rowb, colb):
    y, z, x, core = net.y, net.z, net.x, net.core
    for b in (0, 1):
        block = direc[:, b * B : (b + 1) * B].astype(BF16)
        rowb[z, x, b] = block
        colb[y, core, b] = block
    lo, hi = pl.ds(0, 32), pl.ds(32, 32)

    def blk(b, first, second):
        return (((z + second) % 4, (x + first) % 4) if b == 0 else ((z + first) % 4, (x + second) % 4)) + (b,)

    firsts, seconds = ("x", "z"), ("z", "x")
    done = []

    def send(ref, device):
        c = net.copy(ref, ref, device)
        done.append(c)
        return c

    one = {}
    for b in (0, 1):
        ref = rowb.at[blk(b, 0, 0)]
        one[b] = [send(ref, net.at(firsts[b], step)) for step in (2, 1, -1)]
    ref = colb.at[y, core]
    col_one = [send(ref, net.at("y", 1)), send(ref, net.at("y", -1))]
    col_core = [send(ref, net.partner())]

    second = {0: {}, 1: {}}

    def spread(b, first):
        ref = rowb.at[blk(b, first, 0)]
        second[b][first] = [send(ref, net.at(seconds[b], 1)), send(ref, net.at(seconds[b], -1))]

    for b in (0, 1):
        spread(b, 0)
    for b in (0, 1):
        one[b][1].wait_recv()
        spread(b, -1)
    for b in (0, 1):
        one[b][2].wait_recv()
        spread(b, 1)
    col_one[0].wait_recv()
    col_two = [send(colb.at[(y + 3) % 4, core, 0], net.at("y", 1))]
    col_one[1].wait_recv()
    col_two.append(send(colb.at[(y + 1) % 4, core, 1], net.at("y", -1)))
    for step in (-1, 1):
        col_core.append(send(colb.at[(y + step) % 4, core], net.partner()))
    last = []

    def relay(b, first):
        up, down = second[b][first]
        up.wait_recv()
        ref = rowb.at[blk(b, first, -1)]
        last.append(send(ref.at[lo], net.at(seconds[b], 1)))
        down.wait_recv()
        ref = rowb.at[blk(b, first, 1)]
        last.append(send(ref.at[hi], net.at(seconds[b], -1)))

    for b in (0, 1):
        one[b][0].wait_recv()
        spread(b, 2)
    for b in (0, 1):
        relay(b, 0)
    for c in col_two:
        c.wait_recv()
    col_core.append(send(colb.at[(y + 2) % 4, core], net.partner()))
    for first in (-1, 1, 2):
        for b in (0, 1):
            relay(b, first)
    for c in last + col_core:
        c.wait_recv()
    for c in done:
        c.wait_send()


class Ring:
    def __init__(self, net, axis, chunk, via, direct, final):
        self.net, self.axis, self.chunk = net, axis, chunk
        self.via, self.direct, self.final = via, direct, final
        self.done = []

    def send(self, src, dst, step):
        c = self.net.copy(src, dst, self.net.at(self.axis, step))
        self.done.append(c)
        return c

    def far(self):
        chunk = self.chunk
        self.one = [self.send(chunk(2, 0), self.via.at[0], 1), self.send(chunk(2, 1), self.via.at[1], -1)]

    def near(self):
        chunk = self.chunk
        self.straight = [
            self.send(chunk(1, 1), self.direct.at[1], 1),
            self.send(chunk(-1, 0), self.direct.at[0], -1),
        ]

    def start(self):
        self.far()
        self.near()

    def forward(self):
        self.two = []
        for half, step in ((0, 1), (1, -1)):
            self.one[half].wait_recv()
            self.via[half] += self.chunk(step, half)[...]
            self.two.append(self.send(self.via.at[half], self.final.at[half], step))

    def result(self, half):
        self.two[half].wait_recv()
        self.straight[1 - half].wait_recv()
        return self.final[half] + self.direct[half]

    def close(self):
        for c in self.done:
            c.wait_send()


def solve(left, right):
    table = jnp.concatenate([left, right], 1)
    row_ids = lax.broadcasted_iota(jnp.int32, (M, 2 * M), 0)
    for k in range(M):
        pivot = table[k : k + 1, :] * (1.0 / table[k : k + 1, k : k + 1])
        table = jnp.where(row_ids == k, pivot, table - table[:, k : k + 1] * pivot)
    return table[:, M:]


def scatter_sums(net, fwd, trans, bufs, beside):
    via_a, dir_a, fin_a, mid, via_b, dir_b, fin_b, core_in, via_y, dir_y, fin_y = bufs
    y, z, x, core = net.y, net.z, net.x, net.core
    half = (pl.ds(0, 32), pl.ds(32, 32))
    axes, order, both = ("x", "z"), (2, 1, -1, 0), (0, 1)
    pos = (z, x)

    def sub(b, s):
        if b == 0:
            return lambda step, h: fwd.at[(z + s) % 4, (x + step) % 4, 0, half[h]]
        return lambda step, h: fwd.at[(z + step) % 4, (x + s) % 4, 1, half[h]]

    rings = {
        (b, s): Ring(net, axes[b], sub(b, s), via_a.at[b, k], dir_a.at[b, k], fin_a.at[b, k])
        for k, s in enumerate(order)
        for b in both
    }
    seconds = [
        Ring(net, axes[1 - b], lambda step, h, b=b: mid.at[b, (pos[b] + step) % 4, half[h]], via_b.at[b], dir_b.at[b], fin_b.at[b])
        for b in both
    ]
    ring_y = Ring(net, "y", lambda step, h: core_in.at[(y + step) % 4, h], via_y, dir_y, fin_y)
    core_copies = {}
    for step in order:
        to = (y + step) % 4
        core_copies[step] = net.copy(trans.at[to, 1 - core], core_in.at[to], net.partner())

    def begin(s):
        for b in both:
            rings[b, s].start()

    def forward(s):
        for b in both:
            rings[b, s].forward()

    def middle(s):
        for b in both:
            at = (pos[b] + s) % 4
            for h in both:
                mid[b, at, h * 32 : h * 32 + 32, :] = sub(b, s)(0, h)[...] + rings[b, s].result(h)

    begin(2)
    begin(1)
    beside[0]()
    for step in order:
        core_copies[step].wait()
        to = (y + step) % 4
        core_in[to] += trans[to, core]
    ring_y.start()
    forward(2)
    begin(-1)
    forward(1)
    begin(0)
    beside[1]()
    middle(2)
    for r in seconds:
        r.far()
    forward(-1)
    ring_y.forward()
    middle(1)
    forward(0)
    middle(-1)
    beside[2]()
    for r in seconds:
        r.near()
        r.forward()
    for b in both:
        ring_y.result(b)
    middle(0)
    for step in beside[3:]:
        step()
    image = []
    for b in both:
        column = core_in[y, b] + (fin_y[b] + dir_y[b])
        parts = [seconds[b].chunk(0, h)[...] + seconds[b].result(h) for h in both]
        image.append(column + jnp.concatenate(parts, 0))
    for r in list(rings.values()) + seconds + [ring_y]:
        r.close()
    return jnp.concatenate(image, 1)


def split3(a):
    high = a.astype(BF16)
    rest = a - high.astype(F32)
    middle = rest.astype(BF16)
    low = (rest - middle.astype(F32)).astype(BF16)
    return jnp.concatenate([high, middle, low], 0)


class Gram:
    def __init__(self, net, fwd, rowb, direc, self_term, own, slots):
        self.net, self.fwd, self.rowb = net, fwd, rowb
        self.direc, self.self_term, self.own, self.slots = direc, self_term, own, slots

    def local(self):
        def step(k, acc):
            for t in range(8):
                q = k * 4 + t // 2
                at = (q // 4, q % 4, t % 2)
                acc = acc + dot(self.rowb[at], split3(self.fwd[at]), NT)
            return acc

        thirds = lax.fori_loop(0, 4, step, jnp.zeros((M, 3 * M), F32))
        h = thirds[:, 0:M] + thirds[:, M : 2 * M] + thirds[:, 2 * M :]
        direc = self.direc[...]
        g = h + h.T + dot(direc * self.self_term[...], direc, NT, HI)
        self.own[0] = jnp.concatenate([g[0:32], g[32:64]], 1)

    def start(self):
        self.copies = [self.net.copy(self.own.at[0], self.slots.at[0, 0], self.net.partner())]

    def stage(self, k):
        wait_all(self.copies)
        got = self.slots[k, 0] if k == 0 else self.slots[k, 0] + self.slots[k, 1] + self.slots[k, 2]
        self.own[k + 1] = self.own[k] + got
        if k < 3:
            self.copies = exchange(self.net, "yxz"[k], self.own.at[k + 1], self.slots.at[k + 1])

    def total(self):
        g = self.own[4]
        return jnp.concatenate([g[:, 0:M], g[:, M:]], 0)


def first_kernel(*refs):
    sources, (direc, rho, proj_out, inner_out, rowb, colb), kept = refs[:6], refs[6:12], refs[12:18]
    part, total, *bufs, send, recv, local_sem = refs[18:]
    rhs, factor, weight = kept[:3]
    copies = [pltpu.make_async_copy(a, b, local_sem.at[k]) for k, (a, b) in enumerate(zip(sources, kept))]
    for c in copies:
        c.start()
    net = Net(send, recv)
    net.greet()
    for c in copies[:3]:
        c.wait()
    resid = rhs[...]
    project(resid, factor, part, [resid])
    net.meet()
    all_reduce_wide(net, part, total, *bufs)
    wide = assemble(total)
    proj, inner = wide[:, 0:D], wide[:, D : D + M]
    precond, rho_value = precondition(resid, proj, inner, factor, weight)
    direc[...] = precond
    gather(net, precond, rowb, colb)
    rho[...] = rho_value
    proj_out[...] = proj
    inner_out[...] = inner
    for c in copies[3:]:
        c.wait()


def middle_kernel(
    fwd, trans, row_in, direc, resid, self_term, rho, proj, inner, factor, weight,
    sol_out, resid_out, direc_out, rho_out, rowb, colb, own, slots, *rest,
):
    bufs, (alpha_ref, turned_ref, part, total, *wide_bufs, send, recv) = rest[:11], rest[11:]
    net = Net(send, recv)
    gram = Gram(net, fwd, row_in, direc, self_term, own, slots)
    net.greet()
    gram.local()
    net.meet()
    gram.start()
    steps = [lambda: gram.stage(0), lambda: gram.stage(1), lambda: gram.stage(2)]
    image = self_term[...] * direc[...] + scatter_sums(net, fwd, trans, bufs, steps)
    project(image, factor, part, [resid[...], image])

    def alpha():
        gram.stage(3)
        g = gram.total()
        alpha_ref[...] = solve((g + g.T) * 0.5, rho[...])

    def update():
        resid_out[...] = resid[...] - dot(alpha_ref[...], image, TN, HI)
        sol_out[...] = dot(alpha_ref[...], direc[...], TN, HI)

    def turn():
        eye = lax.broadcasted_iota(jnp.int32, (M, M), 0) == lax.broadcasted_iota(jnp.int32, (M, M), 1)
        turned_ref[...] = dot(solve(rho[...], eye.astype(F32)), direc[...], TN, HI)

    all_reduce_wide(net, part, total, *wide_bufs, beside=(alpha, update, turn))
    step = alpha_ref[...]
    wide = assemble(total)
    across = dot(step, wide[:, D : D + M], TN, HI)
    own_part = dot(step, dot(wide[:, D + M : D + 2 * M], step, NN, HI), TN, HI)
    new_inner = inner[...] - across - across.T + own_part
    new_proj = proj[...] - dot(step, wide[:, 0:D], TN, HI)
    precond, rho_value = precondition(resid_out[...], new_proj, new_inner, factor, weight)
    fresh = precond + dot(rho_value, turned_ref[...], TN, HI)
    direc_out[...] = fresh
    gather(net, fresh, rowb, colb)
    rho_out[...] = rho_value


def last_kernel(fwd, trans, row_in, direc, resid, sol, self_term, rho, sol_out, resid_out, own, slots, *rest):
    bufs, (alpha_ref, send, recv) = rest[:11], rest[11:]
    net = Net(send, recv)
    gram = Gram(net, fwd, row_in, direc, self_term, own, slots)
    net.greet()
    gram.local()
    net.meet()
    gram.start()

    def alpha():
        gram.stage(3)
        g = gram.total()
        alpha_ref[...] = solve((g + g.T) * 0.5, rho[...])
        sol_out[...] = sol[...] + dot(alpha_ref[...], direc[...], TN, HI)

    steps = [lambda: gram.stage(0), lambda: gram.stage(1), lambda: gram.stage(2), alpha]
    image = self_term[...] * direc[...] + scatter_sums(net, fwd, trans, bufs, steps)
    resid_out[...] = resid[...] - dot(alpha_ref[...], image, TN, HI)


def operate_kernel(*refs):
    sources, (rowb, colb, left, right, tiles, fwd, trans, half_f, half_t), tables, sem = refs[:5], refs[5:14], refs[14:19], refs[19]
    copies = [pltpu.make_async_copy(a, b, sem.at[k]) for k, (a, b) in enumerate(zip(sources, tables))]
    for c in copies:
        c.start()
    fwd[...] = jnp.zeros_like(fwd)
    trans[...] = jnp.zeros_like(trans)
    for c in copies:
        c.wait()
    counts, near_rows, near_cols, far_rows, far_cols = tables
    n = counts[lax.axis_index("row") * lax.axis_size("col") + lax.axis_index("col")]

    def far_halves(k, carry):
        for g in range(16):
            p = k * 16 + g
            half_f[p] = dot(colb[far_cols[p]], right[p], NT).astype(BF16)
            half_t[p] = dot(rowb[far_rows[p]], left[p], NT).astype(BF16)
        return carry

    def far(k, carry):
        out = []
        for g in range(32):
            p = k * 32 + g
            out.append((far_rows[p], far_cols[p], dot(half_f[p], left[p]), dot(half_t[p], right[p])))
        for r, c, f, t in out:
            fwd[r] += f
            trans[c] += t
        return carry

    lax.fori_loop(0, left.shape[0] // 16, far_halves, 0)
    lax.fori_loop(0, left.shape[0] // 32, far, 0)

    def near(k, carry):
        out = []
        for g in range(GROUP):
            s = k * GROUP + g
            r, c = near_rows[s], near_cols[s]
            tile = tiles[s]
            valid = s < n
            f = jnp.where(valid, dot(colb[c], tile, NT), 0.0)
            t = jnp.where(valid, dot(rowb[r], tile), 0.0)
            out.append((r, c, f, t))
        for r, c, f, t in out:
            fwd[r] += f
            trans[c] += t
        return carry

    lax.fori_loop(0, (n + GROUP - 1) // GROUP, near, 0)


def shape(*dims, dtype=F32):
    return jax.ShapeDtypeStruct(dims, dtype)


def wide_scratch():
    v = pltpu.VMEM
    return [
        v((16, 8, CHUNK), F32),
        v((16, 8, CHUNK), F32),
        v((15, 8, CHUNK), F32),
        v((8, CHUNK), F32),
        v((7, 8, CHUNK), F32),
    ]


def scatter_scratch():
    v = pltpu.VMEM
    return (
        [v((5, 32, 128), F32), v((4, 3, 32, 128), F32)]
        + [v((2, 4, 2, 32, B), F32)] * 3
        + [v((2, 4, M, B), F32)]
        + [v((2, 2, 32, B), F32)] * 3
        + [v((4, 2, M, B), F32)]
        + [v((2, M, B), F32)] * 3
    )


def sems(n):
    return [pltpu.SemaphoreType.DMA((n,)), pltpu.SemaphoreType.DMA((n,))]


def params(collective):
    return pltpu.CompilerParams(
        collective_id=collective, has_side_effects=True, vmem_limit_bytes=VMEM_LIMIT
    )


def local(
    rhs, self_term, near_tiles, near_rows, near_cols, near_counts, far_left, far_right, far_rows, far_cols, nys_factor, nys_weight
):
    left, right = jnp.swapaxes(far_left, 1, 2), jnp.swapaxes(far_right, 1, 2)
    weight = nys_weight.reshape(1, -1)
    self_row = self_term.reshape(1, -1)
    row_shape = shape(4, 4, 2, M, B, dtype=BF16)
    col_shape = shape(4, 2, 2, M, B, dtype=BF16)
    n_wide = 15 + 7 + 15
    n_gather = 2 * 3 + 2 * 2 + 4 + 2 * 4 * 2 * 2
    n_scatter = 6 * 8 + 6 * 3 + 4 + 10

    sources = (rhs, nys_factor, weight, near_tiles, left, right)
    direc, rho, proj, inner, rowb, colb, resid, factor, weight, tiles, left, right = pl.pallas_call(
        first_kernel,
        out_shape=(shape(M, D), shape(M, M), shape(M, D), shape(M, M), row_shape, col_shape) + tuple(shape(*a.shape, dtype=a.dtype) for a in sources),
        in_specs=[HBM] * 6,
        out_specs=(VMEM,) * 12,
        scratch_shapes=wide_scratch() + sems(n_wide + n_gather) + [pltpu.SemaphoreType.DMA((6,))],
        compiler_params=params(0),
        name="first",
    )(*[pltpu.with_memory_space_constraint(a, pltpu.HBM) for a in sources])
    tables = (near_counts, near_rows, near_cols, far_rows, far_cols)

    def operate(rowb, colb):
        fwd, trans = pl.pallas_call(
            operate_kernel,
            out_shape=(shape(32, M, B), shape(16, M, B)),
            in_specs=[HBM] * 5 + [VMEM] * 5,
            out_specs=(VMEM, VMEM),
            scratch_shapes=[pltpu.VMEM((far_left.shape[0], M, far_left.shape[2]), BF16)] * 2
            + [pltpu.SMEM(t.shape, jnp.int32) for t in tables]
            + [pltpu.SemaphoreType.DMA((5,))],
            compiler_params=pltpu.CompilerParams(vmem_limit_bytes=VMEM_LIMIT),
            name="operate",
        )(*tables, rowb.reshape(32, M, B), colb.reshape(16, M, B), left, right, tiles)
        return fwd.reshape(4, 4, 2, M, B), trans.reshape(4, 2, 2, M, B)

    fwd, trans = operate(rowb, colb)
    square = pltpu.VMEM((M, M), F32)
    sol, residual, direc, rho_next, rowb, colb = pl.pallas_call(
        middle_kernel,
        out_shape=(shape(M, D), shape(M, D), shape(M, D), shape(M, M), row_shape, col_shape),
        in_specs=[VMEM] * 11,
        out_specs=(VMEM,) * 6,
        scratch_shapes=scatter_scratch() + [square, pltpu.VMEM((M, D), F32)] + wide_scratch() + sems(n_wide + n_gather + n_scatter),
        compiler_params=params(1),
        name="middle",
    )(fwd, trans, rowb, direc, resid, self_row, rho, proj, inner, factor, weight)
    fwd, trans = operate(rowb, colb)
    return pl.pallas_call(
        last_kernel,
        out_shape=(shape(M, D), shape(M, D)),
        in_specs=[VMEM] * 8,
        out_specs=(VMEM,) * 2,
        scratch_shapes=scatter_scratch() + [square] + sems(n_scatter),
        compiler_params=params(2),
        name="last",
    )(fwd, trans, rowb, direc, residual, sol, self_row, rho_next)


def solution(mesh):
    split = ("row", "col")
    in_specs = (
        P(None, split),
        P(split),
        P(split, None, None),
        P(split),
        P(split),
        P(),
        P(split, None, None),
        P(split, None, None),
        P(split),
        P(split),
        P(None, split),
        P(),
    )
    out_specs = (P(None, split), P(None, split))
    return jax.shard_map(local, mesh=mesh, in_specs=in_specs, out_specs=out_specs, check_vma=False)
```

```python
import jax
import jax.numpy as jnp
from jax import lax
from jax.experimental import pallas as pl
from jax.experimental.pallas import tpu as pltpu
from jax.sharding import PartitionSpec as P

MESH = pl.DeviceIdType.MESH
HI = lax.Precision.HIGHEST
F32 = jnp.float32
BF16 = jnp.bfloat16
VMEM = pl.BlockSpec(memory_space=pltpu.VMEM)
SMEM = pl.BlockSpec(memory_space=pltpu.SMEM)
HBM = pl.BlockSpec(memory_space=pltpu.HBM)
NT = (((1,), (1,)), ((), ()))
NN = (((1,), (0,)), ((), ()))
TN = (((0,), (0,)), ((), ()))
M = 64
B = 256
D = 512
CHUNK = 384
GROUP = 16
ROUTED = (2, 1, -1)
VMEM_LIMIT = 16 * 1024 * 1024


def dot(a, b, dims=NN, precision=None):
    return lax.dot_general(a, b, dims, precision=precision, preferred_element_type=F32)


class Net:
    def __init__(self, send, recv):
        self.send, self.recv, self.used = send, recv, 0
        self.i, self.j = lax.axis_index("row"), lax.axis_index("col")
        self.y, self.core = self.i // 2, self.i % 2
        self.z, self.x = self.j // 4, self.j % 4

    def partner(self):
        return (self.y * 2 + 1 - self.core, self.j)

    def at(self, axis, step):
        if axis == "y":
            return ((self.y + step) % 4 * 2 + self.core, self.j)
        if axis == "z":
            return (self.i, (self.z + step) % 4 * 4 + self.x)
        return (self.i, self.z * 4 + (self.x + step) % 4)

    def plane(self):
        steps = [(dz, dx) for dz in (2, 1, 3, 0) for dx in (2, 1, 3, 0)][:-1]
        steps.sort(key=lambda s: -sum(min(d, 4 - d) for d in s))
        return [(self.i, (self.z + dz) % 4 * 4 + (self.x + dx) % 4) for dz, dx in steps]

    def lines(self):
        return [self.at(a, s) for a in "xyz" for s in (2, 1, 3)] + [self.partner()]

    def greet(self, peers):
        self.greeted = len(peers)
        for peer in peers:
            pl.semaphore_signal(pltpu.get_barrier_semaphore(), inc=1, device_id=peer, device_id_type=MESH)

    def meet(self):
        pl.semaphore_wait(pltpu.get_barrier_semaphore(), self.greeted)

    def copy(self, src, dst, device):
        k = self.used
        self.used += 1
        c = pltpu.make_async_remote_copy(
            src_ref=src,
            dst_ref=dst,
            send_sem=self.send.at[k],
            recv_sem=self.recv.at[k],
            device_id=device,
            device_id_type=MESH,
        )
        c.start()
        return c


def rows(start, size):
    return pl.ds(pl.multiple_of(start, 8), size)


def exchange(net, axis, src, slots):
    return [net.copy(src, slots.at[d - 1], net.at(axis, d)) for d in (2, 1, 3)]


def wait_all(copies):
    for c in copies:
        c.wait()


def all_reduce_wide(net, part, total, plane_in, row_own, row_in, row_both, beside=()):
    me = net.j
    copies = [net.copy(part.at[p[1]], plane_in.at[k], p) for k, p in enumerate(net.plane())]
    for step in beside[:1]:
        step()
    wait_all(copies)
    row_own[...] = part[me] + jnp.sum(plane_in[...], 0)
    net.copy(row_own, row_in.at[3], net.partner()).wait()
    row_both[...] = row_own[...] + row_in[3]
    copies = exchange(net, "y", row_both, row_in)
    for step in beside[1:2]:
        step()
    wait_all(copies)
    total[me] = row_both[...] + row_in[0] + row_in[1] + row_in[2]
    copies = [net.copy(total.at[me], total.at[me], p) for p in net.plane()]
    for step in beside[2:]:
        step()
    wait_all(copies)


def project(a, factor, part, others):
    pieces = [dot(a, factor[...], NT, HI)] + [dot(a, o, NT, HI) for o in others]
    used = D + M * len(others)
    wide = jnp.concatenate(pieces + [jnp.zeros((M, 2 * CHUNK - used), F32)], 1)
    for q in range(16):
        part[q] = wide[q // 2 * 8 : q // 2 * 8 + 8, q % 2 * CHUNK : q % 2 * CHUNK + CHUNK]


def assemble(total):
    return jnp.concatenate([jnp.concatenate([total[2 * q], total[2 * q + 1]], 1) for q in range(8)], 0)


def precondition(resid, proj, inner, factor, weight):
    weighted = proj * weight[...]
    precond = resid + dot(weighted, factor[...], NN, HI)
    return precond, inner + dot(weighted, proj, NT, HI)


def gather(net, direc, rowb, colb):
    y, z, x, core = net.y, net.z, net.x, net.core
    for b in (0, 1):
        block = direc[:, b * B : (b + 1) * B].astype(BF16)
        rowb[z, x, b] = block
        colb[y, core, b] = block
    lo, hi = pl.ds(0, 32), pl.ds(32, 32)

    def blk(b, first, second):
        return (((z + second) % 4, (x + first) % 4) if b == 0 else ((z + first) % 4, (x + second) % 4)) + (b,)

    firsts, seconds = ("x", "z"), ("z", "x")
    done = []

    def send(ref, device):
        c = net.copy(ref, ref, device)
        done.append(c)
        return c

    one = {}
    for b in (0, 1):
        ref = rowb.at[blk(b, 0, 0)]
        one[b] = [send(ref, net.at(firsts[b], step)) for step in (2, 1, -1)]
    ref = colb.at[y, core]
    col_one = [send(ref, net.at("y", 1)), send(ref, net.at("y", -1))]
    col_core = [send(ref, net.partner())]

    second = {0: {}, 1: {}}

    def spread(b, first):
        ref = rowb.at[blk(b, first, 0)]
        steps = (2, 1, -1) if first in ROUTED else (1, -1)
        second[b][first] = [send(ref, net.at(seconds[b], step)) for step in steps]

    for b in (0, 1):
        spread(b, 0)
    for b in (0, 1):
        one[b][1].wait_recv()
        spread(b, -1)
    for b in (0, 1):
        one[b][2].wait_recv()
        spread(b, 1)
    col_one[0].wait_recv()
    col_two = [send(colb.at[(y + 3) % 4, core, 0], net.at("y", 1))]
    col_one[1].wait_recv()
    col_two.append(send(colb.at[(y + 1) % 4, core, 1], net.at("y", -1)))
    for step in (-1, 1):
        col_core.append(send(colb.at[(y + step) % 4, core], net.partner()))
    last = []

    def relay(b, first):
        if first in ROUTED:
            last.extend(second[b][first])
            return
        up, down = second[b][first]
        up.wait_recv()
        ref = rowb.at[blk(b, first, -1)]
        last.append(send(ref.at[lo], net.at(seconds[b], 1)))
        down.wait_recv()
        ref = rowb.at[blk(b, first, 1)]
        last.append(send(ref.at[hi], net.at(seconds[b], -1)))

    for b in (0, 1):
        one[b][0].wait_recv()
        spread(b, 2)
    for b in (0, 1):
        relay(b, 0)
    for c in col_two:
        c.wait_recv()
    col_core.append(send(colb.at[(y + 2) % 4, core], net.partner()))
    for first in (-1, 1, 2):
        for b in (0, 1):
            relay(b, first)
    for c in last + col_core:
        c.wait_recv()
    for c in done:
        c.wait_send()


class Ring:
    def __init__(self, net, axis, chunk, via, direct, final):
        self.net, self.axis, self.chunk = net, axis, chunk
        self.via, self.direct, self.final = via, direct, final
        self.done = []

    def send(self, src, dst, step):
        c = self.net.copy(src, dst, self.net.at(self.axis, step))
        self.done.append(c)
        return c

    def far(self):
        chunk = self.chunk
        self.one = [self.send(chunk(2, 0), self.via.at[0], 1), self.send(chunk(2, 1), self.via.at[1], -1)]

    def near(self):
        chunk = self.chunk
        self.straight = [
            self.send(chunk(1, 1), self.direct.at[1], 1),
            self.send(chunk(-1, 0), self.direct.at[0], -1),
        ]

    def start(self):
        self.far()
        self.near()

    def forward(self):
        self.two = []
        for half, step in ((0, 1), (1, -1)):
            self.one[half].wait_recv()
            self.via[half] += self.chunk(step, half)[...]
            self.two.append(self.send(self.via.at[half], self.final.at[half], step))

    def result(self, half):
        self.two[half].wait_recv()
        self.straight[1 - half].wait_recv()
        return self.final[half] + self.direct[half]

    def close(self):
        for c in self.done:
            c.wait_send()


def solve(left, right):
    table = jnp.concatenate([left, right], 1)
    row_ids = lax.broadcasted_iota(jnp.int32, (M, 2 * M), 0)
    for k in range(M):
        pivot = table[k : k + 1, :] * (1.0 / table[k : k + 1, k : k + 1])
        table = jnp.where(row_ids == k, pivot, table - table[:, k : k + 1] * pivot)
    return table[:, M:]


def scatter_sums(net, fwd, trans, bufs, beside):
    via_a, dir_a, fin_a, mid, via_b, dir_b, fin_b, core_in, via_y, dir_y, fin_y = bufs
    y, z, x, core = net.y, net.z, net.x, net.core
    half = (pl.ds(0, 32), pl.ds(32, 32))
    axes, order, both = ("x", "z"), (2, 1, -1, 0), (0, 1)
    pos = (z, x)

    def sub(b, s):
        if b == 0:
            return lambda step, h: fwd.at[(z + s) % 4, (x + step) % 4, 0, half[h]]
        return lambda step, h: fwd.at[(z + step) % 4, (x + s) % 4, 1, half[h]]

    rings = {
        (b, s): Ring(net, axes[b], sub(b, s), via_a.at[b, k], dir_a.at[b, k], fin_a.at[b, k])
        for k, s in enumerate(order)
        for b in both
    }
    seconds = [
        Ring(net, axes[1 - b], lambda step, h, b=b: mid.at[b, (pos[b] + step) % 4, half[h]], via_b.at[b], dir_b.at[b], fin_b.at[b])
        for b in both
    ]
    ring_y = Ring(net, "y", lambda step, h: core_in.at[(y + step) % 4, h], via_y, dir_y, fin_y)
    core_copies = {}
    for step in order:
        to = (y + step) % 4
        core_copies[step] = net.copy(trans.at[to, 1 - core], core_in.at[to], net.partner())

    def begin(s):
        for b in both:
            rings[b, s].start()

    def forward(s):
        for b in both:
            rings[b, s].forward()

    def middle(s):
        for b in both:
            at = (pos[b] + s) % 4
            for h in both:
                mid[b, at, h * 32 : h * 32 + 32, :] = sub(b, s)(0, h)[...] + rings[b, s].result(h)

    begin(2)
    begin(1)
    beside[0]()
    for step in order:
        core_copies[step].wait()
        to = (y + step) % 4
        core_in[to] += trans[to, core]
    ring_y.start()
    forward(2)
    begin(-1)
    forward(1)
    begin(0)
    beside[1]()
    middle(2)
    for r in seconds:
        r.far()
    forward(-1)
    ring_y.forward()
    middle(1)
    forward(0)
    middle(-1)
    beside[2]()
    for r in seconds:
        r.near()
        r.forward()
    for b in both:
        ring_y.result(b)
    middle(0)
    for step in beside[3:]:
        step()
    image = []
    for b in both:
        column = core_in[y, b] + (fin_y[b] + dir_y[b])
        parts = [seconds[b].chunk(0, h)[...] + seconds[b].result(h) for h in both]
        image.append(column + jnp.concatenate(parts, 0))
    for r in list(rings.values()) + seconds + [ring_y]:
        r.close()
    return jnp.concatenate(image, 1)


def split3(a):
    high = a.astype(BF16)
    rest = a - high.astype(F32)
    middle = rest.astype(BF16)
    low = (rest - middle.astype(F32)).astype(BF16)
    return jnp.concatenate([high, middle, low], 0)


class Gram:
    def __init__(self, net, fwd, rowb, direc, self_term, own, slots):
        self.net, self.fwd, self.rowb = net, fwd, rowb
        self.direc, self.self_term, self.own, self.slots = direc, self_term, own, slots

    def local(self):
        def step(k, acc):
            for t in range(8):
                q = k * 4 + t // 2
                at = (q // 4, q % 4, t % 2)
                acc = acc + dot(self.rowb[at], split3(self.fwd[at]), NT)
            return acc

        thirds = lax.fori_loop(0, 4, step, jnp.zeros((M, 3 * M), F32))
        h = thirds[:, 0:M] + thirds[:, M : 2 * M] + thirds[:, 2 * M :]
        direc = self.direc[...]
        g = h + h.T + dot(direc * self.self_term[...], direc, NT, HI)
        self.own[0] = jnp.concatenate([g[0:32], g[32:64]], 1)

    def start(self):
        self.copies = [self.net.copy(self.own.at[0], self.slots.at[0, 0], self.net.partner())]

    def stage(self, k):
        wait_all(self.copies)
        got = self.slots[k, 0] if k == 0 else self.slots[k, 0] + self.slots[k, 1] + self.slots[k, 2]
        self.own[k + 1] = self.own[k] + got
        if k < 3:
            self.copies = exchange(self.net, "yxz"[k], self.own.at[k + 1], self.slots.at[k + 1])

    def total(self):
        g = self.own[4]
        return jnp.concatenate([g[:, 0:M], g[:, M:]], 0)


def first_kernel(*refs):
    sources, (direc, rho, proj_out, inner_out, rowb, colb), kept = refs[:6], refs[6:12], refs[12:18]
    part, total, *bufs, send, recv, local_sem = refs[18:]
    rhs, factor, weight = kept[:3]
    copies = [pltpu.make_async_copy(a, b, local_sem.at[k]) for k, (a, b) in enumerate(zip(sources, kept))]
    for c in copies:
        c.start()
    net = Net(send, recv)
    net.greet(net.plane() + [net.at("y", s) for s in (2, 1, 3)] + [net.partner()])
    for c in copies[:3]:
        c.wait()
    resid = rhs[...]
    project(resid, factor, part, [resid])
    net.meet()
    all_reduce_wide(net, part, total, *bufs)
    wide = assemble(total)
    proj, inner = wide[:, 0:D], wide[:, D : D + M]
    precond, rho_value = precondition(resid, proj, inner, factor, weight)
    direc[...] = precond
    gather(net, precond, rowb, colb)
    rho[...] = rho_value
    proj_out[...] = proj
    inner_out[...] = inner
    for c in copies[3:]:
        c.wait()


def middle_kernel(
    fwd, trans, row_in, direc, resid, self_term, rho, proj, inner, factor, weight,
    sol_out, resid_out, direc_out, rho_out, rowb, colb, own, slots, *rest,
):
    bufs, (alpha_ref, turned_ref, part, total, *wide_bufs, send, recv) = rest[:11], rest[11:]
    net = Net(send, recv)
    gram = Gram(net, fwd, row_in, direc, self_term, own, slots)
    net.greet(net.lines())
    gram.local()
    net.meet()
    gram.start()
    steps = [lambda: gram.stage(0), lambda: gram.stage(1), lambda: gram.stage(2)]
    image = self_term[...] * direc[...] + scatter_sums(net, fwd, trans, bufs, steps)
    project(image, factor, part, [resid[...], image])

    def alpha():
        gram.stage(3)
        g = gram.total()
        alpha_ref[...] = solve((g + g.T) * 0.5, rho[...])

    def update():
        resid_out[...] = resid[...] - dot(alpha_ref[...], image, TN, HI)
        sol_out[...] = dot(alpha_ref[...], direc[...], TN, HI)

    def turn():
        eye = lax.broadcasted_iota(jnp.int32, (M, M), 0) == lax.broadcasted_iota(jnp.int32, (M, M), 1)
        turned_ref[...] = dot(solve(rho[...], eye.astype(F32)), direc[...], TN, HI)

    all_reduce_wide(net, part, total, *wide_bufs, beside=(alpha, update, turn))
    step = alpha_ref[...]
    wide = assemble(total)
    across = dot(step, wide[:, D : D + M], TN, HI)
    own_part = dot(step, dot(wide[:, D + M : D + 2 * M], step, NN, HI), TN, HI)
    new_inner = inner[...] - across - across.T + own_part
    new_proj = proj[...] - dot(step, wide[:, 0:D], TN, HI)
    precond, rho_value = precondition(resid_out[...], new_proj, new_inner, factor, weight)
    fresh = precond + dot(rho_value, turned_ref[...], TN, HI)
    direc_out[...] = fresh
    gather(net, fresh, rowb, colb)
    rho_out[...] = rho_value


def last_kernel(fwd, trans, row_in, direc, resid, sol, self_term, rho, sol_out, resid_out, own, slots, *rest):
    bufs, (alpha_ref, send, recv) = rest[:11], rest[11:]
    net = Net(send, recv)
    gram = Gram(net, fwd, row_in, direc, self_term, own, slots)
    net.greet(net.lines())
    gram.local()
    net.meet()
    gram.start()

    def alpha():
        gram.stage(3)
        g = gram.total()
        alpha_ref[...] = solve((g + g.T) * 0.5, rho[...])
        sol_out[...] = sol[...] + dot(alpha_ref[...], direc[...], TN, HI)

    steps = [lambda: gram.stage(0), lambda: gram.stage(1), lambda: gram.stage(2), alpha]
    image = self_term[...] * direc[...] + scatter_sums(net, fwd, trans, bufs, steps)
    resid_out[...] = resid[...] - dot(alpha_ref[...], image, TN, HI)


def operate_kernel(*refs):
    sources, (rowb, colb, left, right, tiles, fwd, trans, half_f, half_t), tables, sem = refs[:5], refs[5:14], refs[14:19], refs[19]
    copies = [pltpu.make_async_copy(a, b, sem.at[k]) for k, (a, b) in enumerate(zip(sources, tables))]
    for c in copies:
        c.start()
    fwd[...] = jnp.zeros_like(fwd)
    trans[...] = jnp.zeros_like(trans)
    for c in copies:
        c.wait()
    counts, near_rows, near_cols, far_rows, far_cols = tables
    n = counts[lax.axis_index("row") * lax.axis_size("col") + lax.axis_index("col")]

    def far_halves(k, carry):
        for g in range(16):
            p = k * 16 + g
            half_f[p] = dot(colb[far_cols[p]], right[p], NT).astype(BF16)
            half_t[p] = dot(rowb[far_rows[p]], left[p], NT).astype(BF16)
        return carry

    def far(k, carry):
        out = []
        for g in range(32):
            p = k * 32 + g
            out.append((far_rows[p], far_cols[p], dot(half_f[p], left[p]), dot(half_t[p], right[p])))
        for r, c, f, t in out:
            fwd[r] += f
            trans[c] += t
        return carry

    lax.fori_loop(0, left.shape[0] // 16, far_halves, 0)
    lax.fori_loop(0, left.shape[0] // 32, far, 0)

    def near(k, carry):
        out = []
        for g in range(GROUP):
            s = k * GROUP + g
            r, c = near_rows[s], near_cols[s]
            tile = tiles[s]
            valid = s < n
            f = jnp.where(valid, dot(colb[c], tile, NT), 0.0)
            t = jnp.where(valid, dot(rowb[r], tile), 0.0)
            out.append((r, c, f, t))
        for r, c, f, t in out:
            fwd[r] += f
            trans[c] += t
        return carry

    lax.fori_loop(0, (n + GROUP - 1) // GROUP, near, 0)


def shape(*dims, dtype=F32):
    return jax.ShapeDtypeStruct(dims, dtype)


def wide_scratch():
    v = pltpu.VMEM
    return [
        v((16, 8, CHUNK), F32),
        v((16, 8, CHUNK), F32),
        v((15, 8, CHUNK), F32),
        v((8, CHUNK), F32),
        v((4, 8, CHUNK), F32),
        v((8, CHUNK), F32),
    ]


def scatter_scratch():
    v = pltpu.VMEM
    return (
        [v((5, 32, 128), F32), v((4, 3, 32, 128), F32)]
        + [v((2, 4, 2, 32, B), F32)] * 3
        + [v((2, 4, M, B), F32)]
        + [v((2, 2, 32, B), F32)] * 3
        + [v((4, 2, M, B), F32)]
        + [v((2, M, B), F32)] * 3
    )


def sems(n):
    return [pltpu.SemaphoreType.DMA((n,)), pltpu.SemaphoreType.DMA((n,))]


def params(collective):
    return pltpu.CompilerParams(
        collective_id=collective, has_side_effects=True, vmem_limit_bytes=VMEM_LIMIT
    )


def local(
    rhs, self_term, near_tiles, near_rows, near_cols, near_counts, far_left, far_right, far_rows, far_cols, nys_factor, nys_weight
):
    left, right = jnp.swapaxes(far_left, 1, 2), jnp.swapaxes(far_right, 1, 2)
    weight = nys_weight.reshape(1, -1)
    self_row = self_term.reshape(1, -1)
    row_shape = shape(4, 4, 2, M, B, dtype=BF16)
    col_shape = shape(4, 2, 2, M, B, dtype=BF16)
    n_wide = 15 + 4 + 15
    n_gather = 2 * 3 + 2 * 2 + 4 + 2 * (3 * 3 + 4)
    n_scatter = 6 * 8 + 6 * 3 + 4 + 10

    sources = (rhs, nys_factor, weight, near_tiles, left, right)
    direc, rho, proj, inner, rowb, colb, resid, factor, weight, tiles, left, right = pl.pallas_call(
        first_kernel,
        out_shape=(shape(M, D), shape(M, M), shape(M, D), shape(M, M), row_shape, col_shape) + tuple(shape(*a.shape, dtype=a.dtype) for a in sources),
        in_specs=[HBM] * 6,
        out_specs=(VMEM,) * 12,
        scratch_shapes=wide_scratch() + sems(n_wide + n_gather) + [pltpu.SemaphoreType.DMA((6,))],
        compiler_params=params(0),
        name="first",
    )(*[pltpu.with_memory_space_constraint(a, pltpu.HBM) for a in sources])
    tables = (near_counts, near_rows, near_cols, far_rows, far_cols)

    def operate(rowb, colb):
        fwd, trans = pl.pallas_call(
            operate_kernel,
            out_shape=(shape(32, M, B), shape(16, M, B)),
            in_specs=[HBM] * 5 + [VMEM] * 5,
            out_specs=(VMEM, VMEM),
            scratch_shapes=[pltpu.VMEM((far_left.shape[0], M, far_left.shape[2]), BF16)] * 2
            + [pltpu.SMEM(t.shape, jnp.int32) for t in tables]
            + [pltpu.SemaphoreType.DMA((5,))],
            compiler_params=pltpu.CompilerParams(vmem_limit_bytes=VMEM_LIMIT),
            name="operate",
        )(*tables, rowb.reshape(32, M, B), colb.reshape(16, M, B), left, right, tiles)
        return fwd.reshape(4, 4, 2, M, B), trans.reshape(4, 2, 2, M, B)

    fwd, trans = operate(rowb, colb)
    square = pltpu.VMEM((M, M), F32)
    sol, residual, direc, rho_next, rowb, colb = pl.pallas_call(
        middle_kernel,
        out_shape=(shape(M, D), shape(M, D), shape(M, D), shape(M, M), row_shape, col_shape),
        in_specs=[VMEM] * 11,
        out_specs=(VMEM,) * 6,
        scratch_shapes=scatter_scratch() + [square, pltpu.VMEM((M, D), F32)] + wide_scratch() + sems(n_wide + n_gather + n_scatter),
        compiler_params=params(1),
        name="middle",
    )(fwd, trans, rowb, direc, resid, self_row, rho, proj, inner, factor, weight)
    fwd, trans = operate(rowb, colb)
    return pl.pallas_call(
        last_kernel,
        out_shape=(shape(M, D), shape(M, D)),
        in_specs=[VMEM] * 8,
        out_specs=(VMEM,) * 2,
        scratch_shapes=scatter_scratch() + [square] + sems(n_scatter),
        compiler_params=params(2),
        name="last",
    )(fwd, trans, rowb, direc, residual, sol, self_row, rho_next)


def solution(mesh):
    split = ("row", "col")
    in_specs = (
        P(None, split),
        P(split),
        P(split, None, None),
        P(split),
        P(split),
        P(),
        P(split, None, None),
        P(split, None, None),
        P(split),
        P(split),
        P(None, split),
        P(),
    )
    out_specs = (P(None, split), P(None, split))
    return jax.shard_map(local, mesh=mesh, in_specs=in_specs, out_specs=out_specs, check_vma=False)
```
